32 devices in a mesh: gx: 4 (over x, core), gy: 8 (over z, y).
Axes of the slice: x: 2, y: 2, z: 4, core: 2. Of those that a mesh axis runs over, the one named last changes fastest.
Arguments:
- fields: float32 [5, 192, 18432], P(None, 'gx', 'gy'), may hold values from -6 to 6
- winds: float32 [3, 192, 18432], P(None, 'gx', 'gy'), may hold values from -0.1 to 0.1
- diffusion: float32 [192, 18432], P('gx', 'gy'), may hold values from 0.02 to 0.06
- droplets: float32 [16384, 12, 128], P(('gx', 'gy')), may hold values from -3 to 3, as said below
- cells: int32 [16384, 128], P(('gx', 'gy')), may hold values from 0 to 110591, as said below
- balance_list: int32 [16384], P(('gx', 'gy')), may hold values from -1 to 8191, as said below
Outputs:
- fields_out: float32 [5, 192, 18432], P(None, 'gx', 'gy')
- droplets_out: float32 [8192, 12, 128], P(('gx', 'gy'))
The draws below stay inside these ranges and needn't reach their ends.
Inputs may be any that keep to these rules, and one draw needn't show every extreme that they name: `droplets`: Rows: radius in 0.3 to 2, solute term in 0.003 to 0.03, weight in 0.5 to 2, positions and aerosol fractions in 0 to 1, velocities in -3 to 3. `cells`: A cell is (x * 48 + y) * 48 + z in the home tile. All 128 droplets of a block lie in one column (x, y), and within a block the cell never falls. `balance_list`: each home's used entries come first; every value from 0 to 8191 appears exactly once; at most 16 entries of one home name one owner, and some home uses all 512 entries.
All inputs are finite; a program needn't handle non-finite values.
Results may differ from the reference program's by a relative error of at most 0.00011.
Values sent between devices are 32-bit elements; how exact they have to be, the bound alone decides.
A program may use at most 128 MiB of HBM per device.

```python
import math
import jax
import jax.numpy as jnp

CX = 48
CY = 48
NZ = 48
BLOCK = 128
OWN_BLK = 256
SUBSTEPS = 4
HOME_CAP = 512
NX = 192
NY = 384
N_GY = 8
DEVICES = 32


def draw_droplets(key, part):
    key_list = jax.random.split(jax.random.fold_in(key, 3), 6)
    shape_one = (DEVICES * HOME_CAP, 1, BLOCK)
    shape_three = (DEVICES * HOME_CAP, 3, BLOCK)
    radius = jnp.exp(jax.random.uniform(key_list[0], shape_one, jnp.float32, math.log(0.3), math.log(2.0)))
    solute = jnp.exp(jax.random.uniform(key_list[1], shape_one, jnp.float32, math.log(0.003), math.log(0.03)))
    weight = jnp.exp(jax.random.uniform(key_list[2], shape_one, jnp.float32, math.log(0.5), math.log(2.0)))
    velocity = jnp.clip(jax.random.normal(key_list[4], shape_three, jnp.float32), -3.0, 3.0)
    position = jax.random.uniform(key_list[3], shape_three, jnp.float32, 0.0, 1.0)
    aerosol = jax.random.uniform(key_list[5], shape_three, jnp.float32, 0.0, 1.0)
    radius = jnp.clip(radius, 0.3, 2.0)
    solute = jnp.clip(solute, 0.003, 0.03)
    weight = jnp.clip(weight, 0.5, 2.0)
    return jnp.concatenate([radius, solute, weight, position, velocity, aerosol], axis=1).astype(jnp.float32)


def draw_cells(key, part):
    key_list = jax.random.split(jax.random.fold_in(key, 5), 2)
    column_count = CX * CY
    raw_columns = jax.random.randint(key_list[0], (DEVICES, HOME_CAP), 0, column_count)
    raw_columns = raw_columns.at[:, 0].set(0).at[:, -1].set(column_count - 1)
    columns = jnp.sort(raw_columns, axis=1).reshape(DEVICES * HOME_CAP, 1)
    raw_levels = jax.random.randint(key_list[1], (DEVICES * HOME_CAP, BLOCK), 0, NZ)
    raw_levels = raw_levels.at[:, 0].set(0).at[:, -1].set(NZ - 1)
    levels = jnp.sort(raw_levels, axis=1)
    return (columns * NZ + levels).astype(jnp.int32)


def draw_balance_list(key, part):
    key_list = jax.random.split(jax.random.fold_in(key, 7), 3)
    pair_count = DEVICES // 2
    extra = jax.random.randint(key_list[0], (pair_count,), 0, OWN_BLK + 1)
    extra = extra.at[0].set(OWN_BLK)
    ranked = jnp.stack([OWN_BLK + extra, OWN_BLK - extra], axis=1).reshape(-1)
    home_order = jax.random.permutation(key_list[1], DEVICES)
    counts = jnp.zeros((DEVICES,), jnp.int32).at[home_order].set(ranked.astype(jnp.int32))
    starts = jnp.cumsum(counts) - counts
    slot_index = jnp.arange(HOME_CAP, dtype=jnp.int32)
    dealt = starts[:, None] + slot_index[None, :]
    live = slot_index[None, :] < counts[:, None]
    owner_order = jax.random.permutation(key_list[2], DEVICES).astype(jnp.int32)
    target = owner_order[dealt % DEVICES] * OWN_BLK + dealt // DEVICES
    return jnp.where(live, target, -1).reshape(-1).astype(jnp.int32)


def steps_of(own_key, extent, cuts, least, high):
    loudness, own = 1.0, jax.random.fold_in(own_key, 6)
    for dim, parts in cuts:
        steps = jnp.exp(jax.random.uniform(jax.random.fold_in(own, dim), (parts,), jnp.float32, least / len(cuts), high / len(cuts)))
        loudness = loudness * jnp.repeat(steps, extent[dim] // parts).reshape([-1 if axis == dim else 1 for axis in range(len(extent))])
    return loudness


def scatter_about(stream_key, dims, deviation, bound, cuts=(), kind=jnp.bfloat16):
    result = jax.random.normal(stream_key, dims, jnp.float32) * deviation
    if len(cuts) > 0:
        result = steps_of(stream_key, dims, cuts, -0.22, 0.18) * result
    return jnp.clip(result, min=-bound, max=bound).astype(kind)


def setup_inputs(seed: int = 0) -> dict:
    key_of = jax.random.split(jax.random.key(seed), 7)
    return {
        "fields": scatter_about(key_of[0], (5, NX, NY * NZ), 1.0, 6.0, ((1, 4), (2, 8)), jnp.float32),
        "winds": jnp.clip(jax.random.uniform(key_of[1], (3, NX, NY * NZ), jnp.float32, -0.1, 0.1) * steps_of(key_of[1], (3, NX, NY * NZ), ((1, 4), (2, 8)), -0.4, 0.0), -0.1, 0.1),
        "diffusion": jnp.clip(0.02 + 0.04 * jax.random.uniform(key_of[2], (NX, NY * NZ), jnp.float32) ** steps_of(key_of[2], (NX, NY * NZ), ((0, 4), (1, 8)), -0.2, 0.2), 0.02, 0.06),
        "droplets": draw_droplets(jax.random.fold_in(key_of[6], 71), 0),
        "cells": draw_cells(jax.random.fold_in(key_of[6], 71), 0),
        "balance_list": draw_balance_list(jax.random.fold_in(key_of[6], 71), 0),
    }


def face_flux(low_side, high_side, courant_low, courant_high, diff_low, diff_high):
    courant = 0.5 * (courant_low + courant_high)
    diffuse = 0.5 * (diff_low + diff_high)
    return jnp.maximum(courant, 0.0) * low_side + jnp.minimum(courant, 0.0) * high_side - diffuse * (high_side - low_side)

def cell_forcing(theta_cell, vapour_cell):
    supersat = vapour_cell - 0.5 * jnp.tanh(theta_cell)
    growth_rate = 1.0 / (1.0 + 0.1 * theta_cell * theta_cell)
    return (supersat, growth_rate)

def grow(attributes, supersat, growth_rate):
    radius_start = attributes[:, 0]
    solute = attributes[:, 1]
    weight = attributes[:, 2]
    square = radius_start * radius_start
    for substep in range(SUBSTEPS):
        radius = jnp.sqrt(square)
        square = jnp.maximum(square + 0.05 * growth_rate * (supersat - 0.02 / radius + solute / (radius * radius * radius)), 0.04)
    radius = jnp.sqrt(square)
    droplet_mass = weight * (radius * square - radius_start * radius_start * radius_start)
    position = attributes[:, 3:6] + 0.1 * attributes[:, 6:9]
    updated = jnp.concatenate([radius[:, None], attributes[:, 1:3], position, attributes[:, 6:12]], axis=1)
    return (updated, droplet_mass)

def ref_step(state, wind_grid, diff_grid):
    change = jnp.zeros_like(state)
    for axis in range(2):
        ahead = jnp.roll(state, -1, axis + 1)
        courant_here = wind_grid[axis]
        courant_ahead = jnp.roll(courant_here, -1, axis)
        diff_ahead = jnp.roll(diff_grid, -1, axis)
        flux = face_flux(state, ahead, courant_here, courant_ahead, diff_grid, diff_ahead)
        change = change + (flux - jnp.roll(flux, 1, axis + 1))
    flux_z = face_flux(state[..., :-1], state[..., 1:], wind_grid[2][..., :-1], wind_grid[2][..., 1:], diff_grid[..., :-1], diff_grid[..., 1:])
    flux_z = jnp.pad(flux_z, ((0, 0), (0, 0), (0, 0), (1, 1)))
    change = change + (flux_z[..., 1:] - flux_z[..., :-1])
    return state - change

def reference(fields, winds, diffusion, droplets, cells, balance_list):
    grid_shape = (NX, NY, NZ)
    state = fields.reshape((5,) + grid_shape)
    wind_grid = winds.reshape((3,) + grid_shape)
    diff_grid = diffusion.reshape(grid_shape)
    block_count = droplets.shape[0]
    home_tile = jnp.arange(block_count, dtype=jnp.int32) // HOME_CAP
    tile_x = (home_tile // N_GY)[:, None]
    tile_y = (home_tile % N_GY)[:, None]
    local_x = cells // (CY * NZ)
    remain = cells % (CY * NZ)
    local_y = remain // NZ
    local_z = remain % NZ
    global_cell = ((tile_x * CX + local_x) * NY + tile_y * CY + local_y) * NZ + local_z
    global_cell = global_cell.astype(jnp.int32)
    theta_flat = fields[0].reshape(-1)
    vapour_flat = fields[1].reshape(-1)
    supersat, growth_rate = cell_forcing(theta_flat[global_cell], vapour_flat[global_cell])
    updated, grown_mass = grow(droplets, supersat, growth_rate)
    live = balance_list >= 0
    droplet_mass = jnp.where(live[:, None], grown_mass, 0.0)
    condensed = jax.ops.segment_sum(droplet_mass.reshape(-1), global_cell.reshape(-1), num_segments=NX * NY * NZ)
    condensed = condensed.reshape(NX, NY * NZ)
    target = jnp.where(live, balance_list, DEVICES * OWN_BLK).astype(jnp.int32)
    droplets_out = jnp.zeros((DEVICES * OWN_BLK, 12, BLOCK), jnp.float32).at[target].set(updated, mode='drop')
    for substep in range(2):
        state = ref_step(state, wind_grid, diff_grid)
    advanced = state.reshape(5, NX, NY * NZ)
    theta_out = advanced[0] + 0.25 * condensed
    vapour_out = advanced[1] - 0.1 * condensed
    fields_out = jnp.concatenate([theta_out[None], vapour_out[None], advanced[2:5]], axis=0)
    return (fields_out, droplets_out)
```

```python
import jax
import jax.numpy as jnp
from jax import lax
from jax.experimental import pallas as pl
from jax.experimental.pallas import tpu as pltpu
from jax.sharding import PartitionSpec as P

NZ = 48
OWN_BLK = 256
SUBSTEPS = 4
LANES = 128
ROW0 = 16
BATCH = 64
VMEM = pl.BlockSpec(memory_space=pltpu.VMEM)
SMEM = pl.BlockSpec(memory_space=pltpu.SMEM)
LIMIT = 56 * 1024 * 1024


def params():
    return pltpu.CompilerParams(vmem_limit_bytes=LIMIT)


def cost(bytes_accessed, flops):
    return pl.CostEstimate(flops=flops, bytes_accessed=bytes_accessed, transcendentals=0)


OWN_SHIFT = OWN_BLK.bit_length() - 1


def pack_kernel(f_low, f_high, w_low, w_high, d_low, d_high, low_ref, high_ref):
    for f, w, d, out in ((f_low, w_low, d_low, low_ref), (f_high, w_high, d_high, high_ref)):
        out[0:5] = f[...]
        out[5:8] = w[...]
        out[8] = d[...]


def pack_sides(fields, winds, diffusion):
    _, width, merged = fields.shape
    last = merged // LANES - 1
    specs = []
    for count in (5, 3):
        for at in (0, last):
            specs.append(pl.BlockSpec((count, width, LANES), lambda i, at=at: (0, 0, at)))
    for at in (0, last):
        specs.append(pl.BlockSpec((width, LANES), lambda i, at=at: (0, at)))
    shape = jax.ShapeDtypeStruct((9, width, LANES), jnp.float32)
    whole = pl.BlockSpec((9, width, LANES), lambda i: (0, 0, 0))
    return pl.pallas_call(
        pack_kernel,
        grid=(1,),
        out_shape=(shape, shape),
        in_specs=specs,
        out_specs=(whole, whole),
        cost_estimate=cost(1 << 20, 1 << 10),
        name="pack_sides",
    )(fields, fields, winds, winds, diffusion, diffusion)


def split(x):
    high = x.astype(jnp.bfloat16)
    return high, (x - high.astype(jnp.float32)).astype(jnp.bfloat16)


def pick(onehot, x):
    both = jnp.concatenate(split(x), axis=1)
    out = jnp.dot(onehot, both, preferred_element_type=jnp.float32)
    return out[:, :LANES] + out[:, LANES:]


def before_matrix(count):
    row = lax.broadcasted_iota(jnp.int32, (count, count), 0)
    column = lax.broadcasted_iota(jnp.int32, (count, count), 1)
    return jnp.where(row < column, 1.0, 0.0).astype(jnp.bfloat16)


def positions(entries, devices, send_cap):
    home_cap = entries.shape[1]
    owner = jnp.where(entries >= 0, entries >> OWN_SHIFT, devices)
    named = lax.broadcasted_iota(jnp.int32, (devices, home_cap), 0) == owner
    earlier = jnp.dot(
        jnp.where(named, 1.0, 0.0).astype(jnp.bfloat16),
        before_matrix(home_cap),
        preferred_element_type=jnp.float32,
    )
    rank = jnp.sum(jnp.where(named, earlier, 0.0), axis=0, keepdims=True).astype(jnp.int32)
    return jnp.where(entries >= 0, owner * send_cap + rank, devices * send_cap)


def onehot_rows(index, count):
    row = lax.broadcasted_iota(jnp.int32, (count, index.shape[1]), 0)
    return jnp.where(row == index, 1.0, 0.0).astype(jnp.bfloat16)


def pack_kernel_drops(devices, send_cap, entries_ref, drops_ref, moves_ref, out_ref, position_ref, onehot):
    step = pl.program_id(0)

    @pl.when(step == 0)
    def _():
        position = positions(entries_ref[...], devices, send_cap)
        position_ref[...] = position
        onehot[...] = onehot_rows(position, devices * send_cap)

    rate = jnp.where((step >= 2) & (step < 5), 0.1, 0.0)
    packed = pick(onehot[...], drops_ref[0] + rate * moves_ref[0])
    out_ref[...] = packed.reshape(devices, send_cap, LANES)


def pack_drops(entries, planes, devices, send_cap):
    count, home_cap, _ = planes.shape
    total = devices * send_cap
    last = count - 1
    return pl.pallas_call(
        lambda *refs: pack_kernel_drops(devices, send_cap, *refs),
        grid=(count - 1,),
        out_shape=(
            jax.ShapeDtypeStruct((devices, (count - 1) * send_cap, LANES), jnp.float32),
            jax.ShapeDtypeStruct((1, home_cap), jnp.int32),
        ),
        in_specs=[
            pl.BlockSpec((1, home_cap), lambda i: (0, 0)),
            pl.BlockSpec((1, home_cap, LANES), lambda i: (i + 1, 0, 0)),
            pl.BlockSpec((1, home_cap, LANES), lambda i: (jnp.minimum(i + 4, last), 0, 0)),
        ],
        out_specs=(
            pl.BlockSpec((devices, send_cap, LANES), lambda i: (0, i, 0)),
            pl.BlockSpec((1, home_cap), lambda i: (0, 0)),
        ),
        scratch_shapes=[pltpu.VMEM((total, home_cap), jnp.bfloat16)],
        compiler_params=pltpu.CompilerParams(vmem_limit_bytes=24 * 1024 * 1024),
        cost_estimate=cost(6 << 20, 1 << 20),
        name="pack_drops",
    )(entries, planes, planes)


def codes_kernel(send_cap, me_ref, lists_ref, out_ref):
    homes, home_cap = lists_ref.shape
    entries = lists_ref[...]
    mine = (entries >= 0) & ((entries >> OWN_SHIFT) == me_ref[0])
    earlier = jnp.dot(
        jnp.where(mine, 1.0, 0.0).astype(jnp.bfloat16),
        before_matrix(home_cap),
        preferred_element_type=jnp.float32,
    )
    rank = jnp.where(mine, earlier.astype(jnp.int32), send_cap)
    slot = ((entries & (OWN_BLK - 1)) + 1).astype(jnp.float32)
    lane = lax.broadcasted_iota(jnp.int32, (homes, homes * send_cap), 1)
    home = lax.broadcasted_iota(jnp.int32, (homes, homes * send_cap), 0)
    spread = jnp.zeros((homes, homes * send_cap), jnp.float32)
    for i in range(send_cap):
        code = jnp.sum(jnp.where(rank == i, slot, 0.0), axis=1, keepdims=True)
        spread = jnp.where(lane == home * send_cap + i, code, spread)
    out_ref[...] = jnp.sum(spread, axis=0, keepdims=True).astype(jnp.int32) - 1


def arrival_codes(me, lists, send_cap):
    homes = lists.shape[0]
    return pl.pallas_call(
        lambda *refs: codes_kernel(send_cap, *refs),
        out_shape=jax.ShapeDtypeStruct((1, homes * send_cap), jnp.int32),
        in_specs=[SMEM, VMEM],
        out_specs=VMEM,
        cost_estimate=cost(1 << 18, 1 << 22),
        name="arrival_codes",
    )(me, lists)


def place_kernel(codes_ref, arrived_ref, radius_ref, out_ref, onehot):
    step = pl.program_id(0)
    total = codes_ref.shape[1]

    @pl.when(step == 0)
    def _():
        onehot[...] = onehot_rows(codes_ref[...], OWN_BLK)
        out_ref[0] = pick(onehot[...], radius_ref[...].reshape(total, LANES))

    @pl.when(step > 0)
    def _():
        out_ref[0] = pick(onehot[...], arrived_ref[...].reshape(total, LANES))


def place_drops(codes, arrived, radius, count):
    devices, send_cap, _ = radius.shape
    total = devices * send_cap
    return pl.pallas_call(
        place_kernel,
        grid=(count,),
        out_shape=jax.ShapeDtypeStruct((count, OWN_BLK, LANES), jnp.float32),
        in_specs=[
            pl.BlockSpec((1, total), lambda i: (0, 0)),
            pl.BlockSpec((devices, send_cap, LANES), lambda i: (0, jnp.maximum(i - 1, 0), 0)),
            pl.BlockSpec((devices, send_cap, LANES), lambda i: (0, 0, 0)),
        ],
        out_specs=pl.BlockSpec((1, OWN_BLK, LANES), lambda i: (i, 0, 0)),
        scratch_shapes=[pltpu.VMEM((OWN_BLK, total), jnp.bfloat16)],
        compiler_params=pltpu.CompilerParams(vmem_limit_bytes=16 * 1024 * 1024),
        cost_estimate=cost(5 << 20, 1 << 20),
        name="place_drops",
    )(codes, arrived, radius)


def grow_kernel(
    home_cap,
    column_ref,
    source_ref,
    live_ref,
    table_ref,
    level_ref,
    drops_ref,
    cond_ref,
    sent_ref,
    picked,
    radius_out,
    mass,
):
    live_count = live_ref[0]

    def fetch(g, carry):
        for i in range(8):
            b = g * 8 + i
            picked[pl.ds(b, 1), :] = table_ref[pl.ds(column_ref[b], 1), :]
        return carry

    lax.fori_loop(0, home_cap // 8, fetch, 0)

    def one(g, carry):
        at = pl.multiple_of(g * BATCH, BATCH)
        rows = pl.ds(at, BATCH)
        level = level_ref[rows, :]
        pair = picked[rows, :]
        theta = jnp.take_along_axis(pair, level, axis=1)
        vapour = jnp.take_along_axis(pair, level + 64, axis=1)
        supersat = vapour - 0.5 * jnp.tanh(theta)
        growth_rate = 1.0 / (1.0 + 0.1 * theta * theta)
        start = drops_ref[rows, :]
        solute = drops_ref[pl.ds(home_cap + at, BATCH), :]
        weight = drops_ref[pl.ds(2 * home_cap + at, BATCH), :]
        square = start * start
        for _ in range(SUBSTEPS):
            radius = jnp.sqrt(square)
            square = jnp.maximum(
                square
                + 0.05
                * growth_rate
                * (supersat - 0.02 / radius + solute / (radius * radius * radius)),
                0.04,
            )
        radius = jnp.sqrt(square)
        radius_out[rows, :] = radius
        grown = weight * (radius * square - start * start * start)
        block = at + lax.broadcasted_iota(jnp.int32, (BATCH, LANES), 0)
        mass[rows, :] = jnp.where(block < live_count, grown, 0.0)
        return carry

    lax.fori_loop(0, home_cap // BATCH, one, 0)

    total = sent_ref.shape[0]
    sent_ref[...] = pick(onehot_rows(source_ref[...], total), radius_out[...])
    row = lax.broadcasted_iota(jnp.int32, (LANES, LANES), 0)
    column = lax.broadcasted_iota(jnp.int32, (LANES, LANES), 1)
    upper = (row <= column).astype(jnp.float32)
    mass[...] = jnp.dot(
        mass[...], upper, precision=lax.Precision.HIGHEST, preferred_element_type=jnp.float32
    )
    cond_ref[...] = jnp.zeros_like(cond_ref)
    lane = lax.broadcasted_iota(jnp.int32, (BATCH, LANES), 1)

    def sums(g, carry):
        rows = pl.ds(pl.multiple_of(g * BATCH, BATCH), BATCH)
        level = level_ref[rows, :]
        count = jnp.zeros((BATCH, LANES), jnp.int32)
        step = LANES
        while step >= 1:
            probe = jnp.minimum(count + (step - 1), LANES - 1)
            below = jnp.take_along_axis(level, probe, axis=1) <= lane
            count = jnp.where(below & (count + step <= LANES), count + step, count)
            step //= 2
        upto = jnp.take_along_axis(mass[rows, :], jnp.maximum(count - 1, 0), axis=1)
        upto = jnp.where(count > 0, upto, 0.0)
        before = jnp.where(lane == 0, 0.0, pltpu.roll(upto, 1, 1))
        picked[rows, :] = upto - before
        return carry

    lax.fori_loop(0, home_cap // BATCH, sums, 0)

    def scatter(g, carry):
        for i in range(8):
            b = g * 8 + i
            at = pl.ds(column_ref[b], 1)
            cond_ref[at, :] = cond_ref[at, :] + picked[pl.ds(b, 1), :]
        return carry

    lax.fori_loop(0, home_cap // 8, scatter, 0)


def grow_blocks(column, source, live_count, table, level, planes, total):
    home_cap = level.shape[0]
    scratch = pltpu.VMEM((home_cap, LANES), jnp.float32)
    return pl.pallas_call(
        lambda *refs: grow_kernel(home_cap, *refs),
        out_shape=(
            jax.ShapeDtypeStruct(table.shape, jnp.float32),
            jax.ShapeDtypeStruct((total, LANES), jnp.float32),
        ),
        in_specs=[SMEM, VMEM, SMEM, VMEM, VMEM, VMEM],
        out_specs=(VMEM, VMEM),
        scratch_shapes=[scratch, scratch, scratch],
        compiler_params=params(),
        cost_estimate=cost(8 << 20, 1 << 24),
        name="grow_blocks",
    )(column, source, live_count, table, level, planes)


def stencil_kernel(
    fields_ref,
    winds_ref,
    diff_ref,
    low_x,
    high_x,
    low_y,
    high_y,
    cond_ref,
    out_ref,
    ext,
    mid,
    coef,
):
    width = fields_ref.shape[1]
    merged = fields_ref.shape[2]
    lanes = merged + 2 * LANES
    core = slice(LANES, LANES + merged)
    inner = slice(ROW0, ROW0 + width)
    for k in range(9):
        if k < 5:
            own = fields_ref[k]
        elif k < 8:
            own = winds_ref[k - 5]
        else:
            own = diff_ref[...]
        ext[k, inner, core] = own
        ext[k, ROW0 - 2 : ROW0, :] = low_x[k]
        ext[k, ROW0 + width : ROW0 + width + 2, :] = high_x[k]
        ext[k, inner, 0:LANES] = low_y[k]
        ext[k, inner, LANES + merged : lanes] = high_y[k]

    chunks = range(ROW0 - 8, ROW0 + width + 8, 8)
    z = (lax.broadcasted_iota(jnp.int32, (8, lanes), 1) + (NZ - LANES % NZ)) % NZ
    top = z == NZ - 1
    bottom = z == 0

    def faces(c_low, c_high, k_low, k_high):
        courant = 0.5 * (c_low + c_high)
        diffuse = 0.5 * (k_low + k_high)
        return jnp.maximum(courant, 0.0) + diffuse, jnp.minimum(courant, 0.0) - diffuse

    def ahead(v, n):
        return pltpu.roll(v, lanes - n, 1)

    def behind(v, n):
        return pltpu.roll(v, n, 1)

    for base in chunks:
        rows = slice(base, base + 8)
        up = slice(base + 1, base + 9)
        down = slice(base - 1, base + 7)
        k0 = ext[8, rows, :]
        u0 = ext[5, rows, :]
        p, n = faces(u0, ext[5, up, :], k0, ext[8, up, :])
        p_low, n_low = faces(ext[5, down, :], u0, ext[8, down, :], k0)
        centre = 1.0 - (p - n_low)
        coef[0, rows, :] = -n
        coef[1, rows, :] = p_low
        v0 = ext[6, rows, :]
        p, n = faces(v0, ahead(v0, NZ), k0, ahead(k0, NZ))
        centre = centre - (p - behind(n, NZ))
        coef[2, rows, :] = -n
        coef[3, rows, :] = behind(p, NZ)
        w0 = ext[7, rows, :]
        p, n = faces(w0, ahead(w0, 1), k0, ahead(k0, 1))
        p = jnp.where(top, 0.0, p)
        n = jnp.where(top, 0.0, n)
        coef[4, rows, :] = -n
        p_low = jnp.where(bottom, 0.0, behind(p, 1))
        n_low = jnp.where(bottom, 0.0, behind(n, 1))
        coef[5, rows, :] = p_low
        coef[6, rows, :] = centre - (p - n_low)

    def update(src, f, base):
        rows = slice(base, base + 8)
        mine = src[f, rows, :]
        new = coef[6, rows, :] * mine
        new += coef[0, rows, :] * src[f, base + 1 : base + 9, :]
        new += coef[1, rows, :] * src[f, base - 1 : base + 7, :]
        new += coef[2, rows, :] * ahead(mine, NZ)
        new += coef[3, rows, :] * behind(mine, NZ)
        new += coef[4, rows, :] * ahead(mine, 1)
        new += coef[5, rows, :] * behind(mine, 1)
        return new

    def first(f, carry):
        for base in chunks:
            mid[f, base : base + 8, :] = update(ext, f, base)
        return carry

    lax.fori_loop(0, 5, first, 0)

    def second(f, carry):
        share = jnp.where(f == 0, 0.25, jnp.where(f == 1, -0.1, 0.0))
        for base in range(ROW0, ROW0 + width, 8):
            at = slice(base - ROW0, base - ROW0 + 8)
            out_ref[f, at, :] = update(mid, f, base)[:, core] + share * cond_ref[at, :]
        return carry

    lax.fori_loop(0, 5, second, 0)


def advance(fields, winds, diffusion, low_x, high_x, low_y, high_y, condensed):
    _, width, merged = fields.shape
    tall = ROW0 + width + 16
    wide = merged + 2 * LANES
    return pl.pallas_call(
        stencil_kernel,
        out_shape=jax.ShapeDtypeStruct(fields.shape, jnp.float32),
        in_specs=[VMEM] * 8,
        out_specs=VMEM,
        scratch_shapes=[
            pltpu.VMEM((9, tall, wide), jnp.float32),
            pltpu.VMEM((5, tall, wide), jnp.float32),
            pltpu.VMEM((7, tall, wide), jnp.float32),
        ],
        compiler_params=params(),
        cost_estimate=cost(16 << 20, 1 << 26),
        name="advance",
    )(fields, winds, diffusion, low_x, high_x, low_y, high_y, condensed)


def both_ways(low_edge, high_edge, axis):
    count = lax.axis_size(axis)
    return (
        lax.ppermute(high_edge, axis, [(i, (i + 1) % count) for i in range(count)]),
        lax.ppermute(low_edge, axis, [((i + 1) % count, i) for i in range(count)]),
    )


def per_device(fields, winds, diffusion, droplets, cells, balance_list):
    width = fields.shape[1]
    merged = fields.shape[2]
    home_cap = balance_list.shape[0]
    devices = lax.axis_size(("gx", "gy"))
    send_cap = -(-(home_cap // devices) // 8) * 8
    count = droplets.shape[1]
    column_count = width * merged // NZ
    everyone = ("gx", "gy")
    planes = droplets.transpose(1, 0, 2)

    def exchange(x):
        return lax.all_to_all(x, everyone, split_axis=0, concat_axis=0, tiled=True)

    outgoing, position = pack_drops(
        balance_list.reshape(1, home_cap), planes, devices, send_cap
    )
    outgoing, position, fields, winds, diffusion, cells, balance_list = lax.optimization_barrier(
        (outgoing, position, fields, winds, diffusion, cells, balance_list)
    )
    arrived = exchange(outgoing)
    sides = pack_sides(fields, winds, diffusion)
    low_y, high_y = both_ways(*sides, "gy")
    lists = lax.all_gather(balance_list, everyone)
    live_count = jnp.sum((balance_list >= 0).astype(jnp.int32))[None]

    def edge(xs):
        grids = (fields, winds, diffusion[None])
        own = jnp.concatenate([g[:, xs] for g in grids], axis=0)
        return jnp.concatenate([low_y[:, xs], own, high_y[:, xs]], axis=2)

    x_edges = (edge(slice(0, 2)), edge(slice(width - 2, width)))
    x_edges, cells, fields = lax.optimization_barrier((x_edges, cells, fields))
    column = cells[:, 0] // NZ
    low_x, high_x = both_ways(*x_edges, "gx")

    level = cells % NZ
    gap = jnp.zeros((column_count, LANES // 2 - NZ), jnp.float32)
    table = jnp.concatenate(
        [
            fields[0].reshape(column_count, NZ),
            gap,
            fields[1].reshape(column_count, NZ),
            gap,
        ],
        axis=1,
    )
    condensed, radius = grow_blocks(
        column,
        position,
        live_count,
        table,
        level,
        planes.reshape(count * home_cap, LANES),
        devices * send_cap,
    )
    codes = arrival_codes(lax.axis_index(everyone).reshape(1), lists, send_cap)
    condensed = condensed[:, :NZ].reshape(width, merged)
    fields_out = advance(fields, winds, diffusion, low_x, high_x, low_y, high_y, condensed)

    arrived, radius, fields_out, codes = lax.optimization_barrier(
        (arrived, radius, fields_out, codes)
    )
    arrived_radius = exchange(radius.reshape(devices, send_cap, LANES))
    placed = place_drops(codes, arrived, arrived_radius, count)
    droplets_out = placed.transpose(1, 0, 2)
    return (fields_out, droplets_out)


def solution(mesh):
    return jax.shard_map(
        per_device,
        mesh=mesh,
        in_specs=(
            P(None, "gx", "gy"),
            P(None, "gx", "gy"),
            P("gx", "gy"),
            P(("gx", "gy"), None, None),
            P(("gx", "gy"), None),
            P(("gx", "gy")),
        ),
        out_specs=(P(None, "gx", "gy"), P(("gx", "gy"), None, None)),
        check_vma=False,
    )
```

```python
import math

import jax
import jax.numpy as jnp
from jax import lax
from jax.experimental import pallas as pl
from jax.experimental.pallas import tpu as pltpu
from jax.sharding import PartitionSpec as P

NZ = 48
OWN_BLK = 256
SUBSTEPS = 4
LANES = 128
ROW0 = 16
BATCH = 64
OWN_SHIFT = OWN_BLK.bit_length() - 1
GROUP = math.lcm(NZ, LANES)
SPAN = GROUP // LANES
DIRECT = 8
ROOM = 40
CHUNKS = ((9, 10, 11), (1, 2, 6, 7), (8, 3, 4, 5), (0,))
LOADS = ((9, 3), (0, 3), (3, 6))
VMEM = pl.BlockSpec(memory_space=pltpu.VMEM)
SMEM = pl.BlockSpec(memory_space=pltpu.SMEM)
ANY = pl.BlockSpec(memory_space=pl.ANY)
MESH = pl.DeviceIdType.MESH
LIMIT = 56 * 1024 * 1024


def cost(bytes_accessed, flops):
    return pl.CostEstimate(flops=flops, bytes_accessed=bytes_accessed, transcendentals=0)


def split(x):
    high = x.astype(jnp.bfloat16)
    return high, (x - high.astype(jnp.float32)).astype(jnp.bfloat16)


def pick(onehot, x):
    both = jnp.concatenate(split(x), axis=1)
    out = jnp.dot(onehot, both, preferred_element_type=jnp.float32)
    return out[:, :LANES] + out[:, LANES:]


def before_matrix(count):
    row = lax.broadcasted_iota(jnp.int32, (count, count), 0)
    column = lax.broadcasted_iota(jnp.int32, (count, count), 1)
    return jnp.where(row < column, 1.0, 0.0).astype(jnp.bfloat16)


def positions(entries, devices, send_cap):
    home_cap = entries.shape[1]
    owner = jnp.where(entries >= 0, entries >> OWN_SHIFT, devices)
    named = lax.broadcasted_iota(jnp.int32, (devices, home_cap), 0) == owner
    earlier = jnp.dot(
        jnp.where(named, 1.0, 0.0).astype(jnp.bfloat16),
        before_matrix(home_cap),
        preferred_element_type=jnp.float32,
    )
    rank = jnp.sum(jnp.where(named, earlier, 0.0), axis=0, keepdims=True).astype(jnp.int32)
    return jnp.where(entries >= 0, owner * send_cap + rank, devices * send_cap)


def onehot_rows(index, count):
    row = lax.broadcasted_iota(jnp.int32, (count, index.shape[1]), 0)
    return jnp.where(row == index, 1.0, 0.0).astype(jnp.bfloat16)


def pack_kernel(devices, send_cap, entries_ref, drops_ref, moves_ref, out_ref, onehot):
    step = pl.program_id(0)

    @pl.when(step == 0)
    def _():
        position = positions(entries_ref[...], devices, send_cap)
        onehot[...] = onehot_rows(position, devices * send_cap)

    rate = jnp.where((step >= 2) & (step < 5), 0.1, 0.0)
    packed = pick(onehot[...], drops_ref[0] + rate * moves_ref[0])
    out_ref[...] = packed.reshape(devices, send_cap, LANES)


def pack_drops(entries, planes, devices, send_cap):
    count, home_cap, _ = planes.shape
    total = devices * send_cap
    last = count - 1
    return pl.pallas_call(
        lambda *refs: pack_kernel(devices, send_cap, *refs),
        grid=(count - 1,),
        out_shape=jax.ShapeDtypeStruct((devices, (count - 1) * send_cap, LANES), jnp.float32),
        in_specs=[
            pl.BlockSpec((1, home_cap), lambda i: (0, 0)),
            pl.BlockSpec((1, home_cap, LANES), lambda i: (i + 1, 0, 0)),
            pl.BlockSpec((1, home_cap, LANES), lambda i: (jnp.minimum(i + 4, last), 0, 0)),
        ],
        out_specs=pl.BlockSpec((devices, send_cap, LANES), lambda i: (0, i, 0)),
        scratch_shapes=[pltpu.VMEM((total, home_cap), jnp.bfloat16)],
        compiler_params=pltpu.CompilerParams(vmem_limit_bytes=24 * 1024 * 1024),
        cost_estimate=cost(6 << 20, 1 << 20),
        name="pack_drops",
    )(entries, planes, planes)


def codes_kernel(send_cap, me_ref, lists_ref, out_ref):
    homes, home_cap = lists_ref.shape
    entries = lists_ref[...]
    mine = (entries >= 0) & ((entries >> OWN_SHIFT) == me_ref[0])
    earlier = jnp.dot(
        jnp.where(mine, 1.0, 0.0).astype(jnp.bfloat16),
        before_matrix(home_cap),
        preferred_element_type=jnp.float32,
    )
    rank = jnp.where(mine, earlier.astype(jnp.int32), send_cap)
    slot = ((entries & (OWN_BLK - 1)) + 1).astype(jnp.float32)
    lane = lax.broadcasted_iota(jnp.int32, (homes, homes * send_cap), 1)
    home = lax.broadcasted_iota(jnp.int32, (homes, homes * send_cap), 0)
    spread = jnp.zeros((homes, homes * send_cap), jnp.float32)
    for i in range(send_cap):
        code = jnp.sum(jnp.where(rank == i, slot, 0.0), axis=1, keepdims=True)
        spread = jnp.where(lane == home * send_cap + i, code, spread)
    out_ref[...] = jnp.sum(spread, axis=0, keepdims=True).astype(jnp.int32) - 1


def arrival_codes(me, lists, send_cap):
    homes = lists.shape[0]
    return pl.pallas_call(
        lambda *refs: codes_kernel(send_cap, *refs),
        out_shape=jax.ShapeDtypeStruct((1, homes * send_cap), jnp.int32),
        in_specs=[SMEM, VMEM],
        out_specs=VMEM,
        cost_estimate=cost(1 << 18, 1 << 22),
        name="arrival_codes",
    )(me, lists)


def place_kernel(codes_ref, arrived_ref, out_ref, onehot):
    total = codes_ref.shape[1]

    @pl.when(pl.program_id(0) == 0)
    def _():
        onehot[...] = onehot_rows(codes_ref[...], OWN_BLK)

    out_ref[0] = pick(onehot[...], arrived_ref[...].reshape(total, LANES))


def place_drops(codes, arrived, count):
    total = codes.shape[1]
    devices = arrived.shape[0]
    send_cap = total // devices
    return pl.pallas_call(
        place_kernel,
        grid=(count,),
        out_shape=jax.ShapeDtypeStruct((count, OWN_BLK, LANES), jnp.float32),
        in_specs=[
            pl.BlockSpec((1, total), lambda i: (0, 0)),
            pl.BlockSpec((devices, send_cap, LANES), lambda i: (0, (i + count - 1) % count, 0)),
        ],
        out_specs=pl.BlockSpec((1, OWN_BLK, LANES), lambda i: (i, 0, 0)),
        scratch_shapes=[pltpu.VMEM((OWN_BLK, total), jnp.bfloat16)],
        compiler_params=pltpu.CompilerParams(vmem_limit_bytes=16 * 1024 * 1024),
        cost_estimate=cost(5 << 20, 1 << 20),
        name="place_drops",
    )(codes, arrived)

class Plan:
    def __init__(self, axes, home_cap, width, merged):
        self.across, self.along = axes
        self.devices = self.across * self.along
        self.home_cap = home_cap
        self.width, self.merged = width, merged
        self.cap = -(-(home_cap // self.devices) // 8) * 8
        self.direct = min(DIRECT, self.cap)
        self.extra = self.cap - self.direct
        self.low = 2 if self.along % 2 == 0 else 1
        self.levels = self.along // self.low
        self.places = self.across * self.low
        self.room = min(ROOM, self.places * self.extra)
        self.slots = self.devices * self.cap
        arrivals = self.devices * self.direct
        if self.extra:
            arrivals += self.places * self.extra + self.levels * self.room
        self.arrivals = arrivals
        self.padded = -(-arrivals // LANES) * LANES


def quot(v, by):
    return ((v.astype(jnp.float32) + 0.5) * (1.0 / by)).astype(jnp.int32)


def device_parts(plan, d):
    gx = quot(d, plan.along)
    gy = d - gx * plan.along
    level = quot(gy, plan.low)
    place = gx * plan.low + (gy - level * plan.low)
    return level, place


def send_positions(plan, entries):
    home_cap = plan.home_cap
    live = entries >= 0
    owner = jnp.where(live, entries >> OWN_SHIFT, plan.devices)
    named = lax.broadcasted_iota(jnp.int32, (plan.devices, home_cap), 0) == owner
    earlier = jnp.dot(
        jnp.where(named, 1.0, 0.0).astype(jnp.bfloat16),
        before_matrix(home_cap),
        preferred_element_type=jnp.float32,
    )
    rank = jnp.sum(jnp.where(named, earlier, 0.0), axis=0, keepdims=True).astype(jnp.int32)
    position = owner * plan.direct + rank
    if plan.extra:
        level, place = device_parts(plan, owner)
        later = (
            plan.devices * plan.direct
            + (place * plan.levels + level) * plan.extra
            + rank
            - plan.direct
        )
        position = jnp.where(rank < plan.direct, position, later)
    return jnp.where(live, position, plan.slots)


def column_sum(x):
    return jnp.sum(x, axis=1, keepdims=True)


def same_level_before(plan):
    shape = (plan.devices, plan.devices)
    level_r, place_r = device_parts(plan, lax.broadcasted_iota(jnp.int32, shape, 0))
    level_c, place_c = device_parts(plan, lax.broadcasted_iota(jnp.int32, shape, 1))
    return jnp.where((level_r == level_c) & (place_c < place_r), 1.0, 0.0).astype(jnp.bfloat16)


def extra_start(plan, before, over):
    wide = jnp.broadcast_to(over, (plan.devices, LANES)).astype(jnp.bfloat16)
    start = jnp.dot(before, wide, preferred_element_type=jnp.float32)
    return start[:, 0:1]


def arrival_matrix(plan, lists, me, my_level):
    devices, home_cap, direct = plan.devices, plan.home_cap, plan.direct
    mine = (lists >= 0) & ((lists >> OWN_SHIFT) == me)
    flags = jnp.where(mine, 1.0, 0.0)
    earlier = jnp.dot(
        flags.astype(jnp.bfloat16), before_matrix(home_cap), preferred_element_type=jnp.float32
    )
    rank = jnp.where(mine, earlier.astype(jnp.int32), plan.cap)
    slot = ((lists & (OWN_BLK - 1)) + 1).astype(jnp.float32)
    home = lax.broadcasted_iota(jnp.int32, (devices, 1), 0)
    if plan.extra:
        over = jnp.maximum(column_sum(flags) - direct, 0.0)
        start = extra_start(plan, same_level_before(plan), over).astype(jnp.int32)
        level, place = device_parts(plan, home)
    lane = lax.broadcasted_iota(jnp.int32, (devices, plan.padded), 1)
    spread = jnp.zeros((devices, plan.padded), jnp.float32)
    for i in range(plan.cap):
        code = column_sum(jnp.where(rank == i, slot, 0.0))
        if i < direct:
            at = home * direct + i
        else:
            near = devices * direct + place * plan.extra + i - direct
            within = start + i - direct
            far = devices * direct + plan.places * plan.extra + level * plan.room + within
            far = jnp.where(within < plan.room, far, plan.padded)
            at = jnp.where(level == my_level, near, far)
        spread = jnp.where((lane == at) & (code > 0.0), code, spread)
    row = jnp.sum(spread, axis=0, keepdims=True).astype(jnp.int32) - 1
    return onehot_rows(row, OWN_BLK)


def relay_matrix(plan, lists, my_level, my_place):
    devices, levels, extra, room = plan.devices, plan.levels, plan.extra, plan.room
    before = same_level_before(plan)
    columns = plan.places * levels * extra
    lane = lax.broadcasted_iota(jnp.int32, (devices, columns), 1)
    lane_place = quot(lane, levels * extra)
    lane_level = quot(lane - lane_place * (levels * extra), extra)
    lane_item = lane - (lane_place * levels + lane_level) * extra
    home = lax.broadcasted_iota(jnp.int32, (devices, 1), 0)
    home_level, home_place = device_parts(plan, home)
    place_gx = my_place // plan.low
    place_gy = my_place % plan.low
    spread = jnp.zeros((devices, columns), jnp.float32)
    for level in range(levels):
        owner = place_gx * plan.along + level * plan.low + place_gy
        named = (lists >= 0) & ((lists >> OWN_SHIFT) == owner)
        over = jnp.maximum(column_sum(jnp.where(named, 1.0, 0.0)) - plan.direct, 0.0)
        start = extra_start(plan, before, over)
        within = start + lane_item.astype(jnp.float32)
        ok = (
            (home_level == my_level)
            & (home_place == lane_place)
            & (lane_level == level)
            & (lane_item.astype(jnp.float32) < over)
            & (within < room)
        )
        spread = jnp.where(ok, within + (level * room + 1), spread)
    row = jnp.sum(spread, axis=0, keepdims=True).astype(jnp.int32) - 1
    return onehot_rows(row, levels * room)


def faces(c_low, c_high, k_low, k_high):
    courant = 0.5 * (c_low + c_high)
    diffuse = 0.5 * (k_low + k_high)
    return jnp.maximum(courant, 0.0) + diffuse, jnp.minimum(courant, 0.0) - diffuse


def stencil(plan, ext, mid, coef, cond_ref, out_ref):
    width, merged = plan.width, plan.merged
    lanes = merged + 2 * LANES
    core = slice(LANES, LANES + merged)
    chunks = range(ROW0 - 8, ROW0 + width + 8, 8)
    z = (lax.broadcasted_iota(jnp.int32, (8, lanes), 1) + (NZ - LANES % NZ)) % NZ
    top = z == NZ - 1
    bottom = z == 0

    def ahead(v, n):
        return pltpu.roll(v, lanes - n, 1)

    def behind(v, n):
        return pltpu.roll(v, n, 1)

    for base in chunks:
        rows = slice(base, base + 8)
        up = slice(base + 1, base + 9)
        down = slice(base - 1, base + 7)
        k0 = ext[8, rows, :]
        u0 = ext[5, rows, :]
        p, n = faces(u0, ext[5, up, :], k0, ext[8, up, :])
        p_low, n_low = faces(ext[5, down, :], u0, ext[8, down, :], k0)
        centre = 1.0 - (p - n_low)
        coef[0, rows, :] = -n
        coef[1, rows, :] = p_low
        v0 = ext[6, rows, :]
        p, n = faces(v0, ahead(v0, NZ), k0, ahead(k0, NZ))
        centre = centre - (p - behind(n, NZ))
        coef[2, rows, :] = -n
        coef[3, rows, :] = behind(p, NZ)
        w0 = ext[7, rows, :]
        p, n = faces(w0, ahead(w0, 1), k0, ahead(k0, 1))
        p = jnp.where(top, 0.0, p)
        n = jnp.where(top, 0.0, n)
        coef[4, rows, :] = -n
        p_low = jnp.where(bottom, 0.0, behind(p, 1))
        n_low = jnp.where(bottom, 0.0, behind(n, 1))
        coef[5, rows, :] = p_low
        coef[6, rows, :] = centre - (p - n_low)

    def update(src, f, base):
        rows = slice(base, base + 8)
        mine = src[f, rows, :]
        new = coef[6, rows, :] * mine
        new += coef[0, rows, :] * src[f, base + 1 : base + 9, :]
        new += coef[1, rows, :] * src[f, base - 1 : base + 7, :]
        new += coef[2, rows, :] * ahead(mine, NZ)
        new += coef[3, rows, :] * behind(mine, NZ)
        new += coef[4, rows, :] * ahead(mine, 1)
        new += coef[5, rows, :] * behind(mine, 1)
        return new

    def first(f, carry):
        for base in chunks:
            mid[f, base : base + 8, :] = update(ext, f, base)
        return carry

    lax.fori_loop(0, 5, first, 0)

    def second(f, carry):
        share = jnp.where(f == 0, 0.25, jnp.where(f == 1, -0.1, 0.0))
        for base in range(ROW0, ROW0 + width, 8):
            at = slice(base - ROW0, base - ROW0 + 8)
            out_ref[f, at, :] = update(mid, f, base)[:, core] + share * cond_ref[at, :]
        return carry

    lax.fori_loop(0, 5, second, 0)


def grow_drops(plan, entries_ref, cells_ref, ext, drops, tab, hot, radius_out, mass, spread):
    width = plan.width
    groups = plan.merged // GROUP
    used = groups * width
    for f in range(2):
        for g in range(groups):
            lanes = slice(LANES + g * GROUP, LANES + (g + 1) * GROUP)
            high, low = split(ext[f, ROW0 : ROW0 + width, lanes])
            tab[g * width : (g + 1) * width, 2 * f * GROUP : (2 * f + 1) * GROUP] = high
            tab[g * width : (g + 1) * width, (2 * f + 1) * GROUP : (2 * f + 2) * GROUP] = low
    if tab.shape[0] > used:
        tab[used:, :] = jnp.zeros((tab.shape[0] - used, tab.shape[1]), jnp.bfloat16)
    live_count = jnp.sum(
        jnp.where(entries_ref[...] >= 0, 1.0, 0.0), axis=1, keepdims=True
    ).astype(jnp.int32)

    def in_group(rows):
        c = cells_ref[rows, :]
        return c, quot(c[:, 0:1], GROUP)

    def one(g, carry):
        at = pl.multiple_of(g * BATCH, BATCH)
        rows = pl.ds(at, BATCH)
        c, q = in_group(rows)
        x = quot(q, groups)
        key = (q - x * groups) * width + x
        lane = lax.broadcasted_iota(jnp.int32, (BATCH, hot.shape[1]), 1)
        chosen = jnp.where(lane == key, 1.0, 0.0).astype(jnp.bfloat16)
        hot[rows, :] = chosen
        both = jnp.dot(chosen, tab[...], preferred_element_type=jnp.float32)
        offset = c - q * GROUP
        part = offset >> 7
        within = offset & (LANES - 1)

        def look(f):
            high = both[:, 2 * f * GROUP : (2 * f + 1) * GROUP]
            value = high + both[:, (2 * f + 1) * GROUP : (2 * f + 2) * GROUP]
            got = jnp.take_along_axis(value[:, :LANES], within, axis=1)
            for t in range(1, SPAN):
                tile = value[:, t * LANES : (t + 1) * LANES]
                got = jnp.where(part == t, jnp.take_along_axis(tile, within, axis=1), got)
            return got

        theta, vapour = look(0), look(1)
        supersat = vapour - 0.5 * jnp.tanh(theta)
        growth_rate = 1.0 / (1.0 + 0.1 * theta * theta)
        start = drops[0, rows, :]
        solute = drops[1, rows, :]
        weight = drops[2, rows, :]
        square = start * start
        for _ in range(SUBSTEPS):
            radius = jnp.sqrt(square)
            square = jnp.maximum(
                square
                + 0.05
                * growth_rate
                * (supersat - 0.02 / radius + solute / (radius * radius * radius)),
                0.04,
            )
        radius = jnp.sqrt(square)
        radius_out[rows, :] = radius
        grown = weight * (radius * square - start * start * start)
        block = at + lax.broadcasted_iota(jnp.int32, (BATCH, LANES), 0)
        mass[rows, :] = jnp.where(block < live_count, grown, 0.0)
        return carry

    lax.fori_loop(0, plan.home_cap // BATCH, one, 0)


def condense(plan, cells_ref, hot, mass, spread, cond):
    width = plan.width
    groups = plan.merged // GROUP
    row = lax.broadcasted_iota(jnp.int32, (LANES, LANES), 0)
    column = lax.broadcasted_iota(jnp.int32, (LANES, LANES), 1)
    upper = (row <= column).astype(jnp.float32)
    mass[...] = jnp.dot(
        mass[...], upper, precision=lax.Precision.HIGHEST, preferred_element_type=jnp.float32
    )
    lane = lax.broadcasted_iota(jnp.int32, (BATCH, LANES), 1)

    def sums(g, carry):
        rows = pl.ds(pl.multiple_of(g * BATCH, BATCH), BATCH)
        c = cells_ref[rows, :]
        offset = c - quot(c[:, 0:1], GROUP) * GROUP
        column = quot(offset[:, 0:1], NZ)
        level = offset - column * NZ
        count = jnp.zeros((BATCH, LANES), jnp.int32)
        step = LANES
        while step >= 1:
            probe = jnp.minimum(count + (step - 1), LANES - 1)
            below = jnp.take_along_axis(level, probe, axis=1) <= lane
            count = jnp.where(below & (count + step <= LANES), count + step, count)
            step //= 2
        upto = jnp.take_along_axis(mass[rows, :], jnp.maximum(count - 1, 0), axis=1)
        upto = jnp.where(count > 0, upto, 0.0)
        before = jnp.where(lane == 0, 0.0, pltpu.roll(upto, 1, 1))
        picked = upto - before
        for t in range(SPAN):
            place = lane + t * LANES
            which = quot(place, NZ)
            here = jnp.take_along_axis(picked, place - which * NZ, axis=1)
            high, low = split(jnp.where(which == column, here, 0.0))
            spread[rows, t * LANES : (t + 1) * LANES] = high
            spread[rows, GROUP + t * LANES : GROUP + (t + 1) * LANES] = low
        return carry

    lax.fori_loop(0, plan.home_cap // BATCH, sums, 0)
    both = lax.dot_general(
        hot[...], spread[...], (((0,), (0,)), ((), ())), preferred_element_type=jnp.float32
    )
    for g in range(groups):
        rows = slice(g * width, (g + 1) * width)
        cond[:, g * GROUP : (g + 1) * GROUP] = both[rows, :GROUP] + both[rows, GROUP:]


def main_kernel(
    plan,
    entries_ref,
    cells_ref,
    fields_hbm,
    winds_hbm,
    diff_hbm,
    planes_hbm,
    fields_out,
    drops_out,
    radius_out,
    flag_out,
    ext,
    mid,
    coef,
    cond,
    drops,
    lists,
    pack_hot,
    relay_hot,
    place_hot,
    tab,
    hot,
    mass,
    spread,
    x_send,
    x_recv,
    load_sem,
    grid_sem,
    list_sem,
    halo_send,
    halo_recv,
    *chunk_refs,
):
    devices, across, along = plan.devices, plan.across, plan.along
    low, levels, places = plan.low, plan.levels, plan.places
    direct, extra, room = plan.direct, plan.extra, plan.room
    width, merged = plan.width, plan.merged
    count = len(CHUNKS)
    per = 6 if extra else 2
    buffers = [chunk_refs[i * per : (i + 1) * per] for i in range(count)]
    sems = chunk_refs[count * per :]
    gx = lax.axis_index("gx")
    gy = lax.axis_index("gy")
    me = gx * along + gy
    my_level = gy // low
    my_place = gx * low + gy % low
    barrier = pltpu.get_barrier_semaphore()

    def device(d):
        return {"gx": d // along, "gy": d % along}

    def greet(s, carry):
        other = (me + s) % devices
        pl.semaphore_signal(barrier, inc=1, device_id=device(other), device_id_type=MESH)
        return carry

    lax.fori_loop(1, devices, greet, 0)

    loads = []
    for i, (at, n) in enumerate(LOADS):
        rows = pl.ds(at, n)
        loads.append(pltpu.make_async_copy(planes_hbm.at[rows], drops.at[rows], load_sem.at[i]))
    own_rows = pl.ds(ROW0, width)
    own_lanes = pl.ds(LANES, merged)
    grids = (
        pltpu.make_async_copy(
            fields_hbm, ext.at[pl.ds(0, 5), own_rows, own_lanes], grid_sem.at[0]
        ),
        pltpu.make_async_copy(winds_hbm, ext.at[pl.ds(5, 3), own_rows, own_lanes], grid_sem.at[1]),
        pltpu.make_async_copy(diff_hbm, ext.at[8, own_rows, own_lanes], grid_sem.at[2]),
    )
    loads[0].start()
    for grid in grids:
        grid.start()
    loads[1].start()
    loads[2].start()

    pack_hot[...] = onehot_rows(send_positions(plan, entries_ref[...]), plan.slots)
    for grid in grids:
        grid.wait()
    pl.semaphore_wait(barrier, devices - 1)

    def remote(src, dst, send_sem, recv_sem, to):
        return pltpu.make_async_remote_copy(
            src_ref=src,
            dst_ref=dst,
            send_sem=send_sem,
            recv_sem=recv_sem,
            device_id=to,
            device_id_type=MESH,
        )

    halos = []

    def halo(src, dst, dx, dy):
        i = len(halos)
        to = {"gx": (gx + dx + across) % across, "gy": (gy + dy + along) % along}
        copy = remote(src, dst, halo_send.at[i], halo_recv.at[i], to)
        copy.start()
        halos.append(copy)

    first_lanes = pl.ds(LANES, LANES)
    last_lanes = pl.ds(merged, LANES)
    left_lanes = pl.ds(0, LANES)
    right_lanes = pl.ds(LANES + merged, LANES)
    every = pl.ds(0, 9)
    halo(ext.at[every, own_rows, first_lanes], ext.at[every, own_rows, right_lanes], 0, -1)
    halo(ext.at[every, own_rows, last_lanes], ext.at[every, own_rows, left_lanes], 0, 1)
    for k in range(9):
        x_send[0, k] = ext[k, ROW0 : ROW0 + 2, LANES : LANES + merged]
        x_send[1, k] = ext[k, ROW0 + width - 2 : ROW0 + width, LANES : LANES + merged]
    begin, end = pl.ds(0, LANES), pl.ds(merged - LANES, LANES)
    both = pl.ds(0, 2)
    for side, dx in ((0, -1), (1, 1)):
        to = x_recv.at[1 - side]
        halo(x_send.at[side], to.at[every, both, own_lanes], dx, 0)
        halo(x_send.at[side, every, both, begin], to.at[every, both, right_lanes], dx, -1)
        halo(x_send.at[side, every, both, end], to.at[every, both, left_lanes], dx, 1)

    def tell(s, carry):
        other = (me + s) % devices
        remote(entries_ref, lists.at[me], list_sem.at[0], list_sem.at[1], device(other)).start()
        return carry

    lax.fori_loop(1, devices, tell, 0)

    def pack(c):
        near, far = buffers[c][0], buffers[c][2] if extra else None
        for r, attribute in enumerate(CHUNKS[c]):
            if attribute == 0:
                value = radius_out[...]
            else:
                value = drops[attribute]
                if 3 <= attribute < 6:
                    value = value + 0.1 * drops[attribute + 3]
            packed = pick(pack_hot[...], value)
            cut = devices * direct
            near[:, r * direct : (r + 1) * direct, :] = packed[:cut].reshape(
                devices, direct, LANES
            )
            if extra:
                n = levels * extra
                far[:, r * n : (r + 1) * n, :] = packed[cut:].reshape(places, n, LANES)

    def send(c):
        near, near_in = buffers[c][0:2]
        if extra:
            far, far_in = buffers[c][2:4]

            def give(s, carry):
                place = (my_place + s) % places
                to = {"gx": place // low, "gy": my_level * low + place % low}
                remote(
                    far.at[place], far_in.at[my_place], sems[2].at[c], sems[3].at[c], to
                ).start()
                return carry

            lax.fori_loop(1, places, give, 0)
            far_in[my_place] = far[my_place]

        def out(s, carry):
            other = (me + s) % devices
            remote(
                near.at[other], near_in.at[me], sems[0].at[c], sems[1].at[c], device(other)
            ).start()
            return carry

        lax.fori_loop(1, devices, out, 0)
        near_in[me] = near[me]

    def wait_all(ref, n, sem):
        part = ref.at[pl.ds(0, n)]
        pltpu.make_async_copy(part, part, sem).wait()

    loads[0].wait()
    pack(0)
    send(0)
    loads[1].wait()
    loads[2].wait()
    pack(1)
    send(1)
    pack(2)
    send(2)
    grow_drops(plan, entries_ref, cells_ref, ext, drops, tab, hot, radius_out, mass, spread)
    pack(3)
    send(3)

    wait_all(lists, devices - 1, list_sem.at[1])
    lists[me] = entries_ref[...]
    known = jnp.concatenate([lists[d] for d in range(devices)], axis=0)
    if extra:
        relay_hot[...] = relay_matrix(plan, known, my_level, my_place)
        for c in range(count):
            far_in, onward, onward_in = buffers[c][3:6]
            wait_all(far_in, places - 1, sems[3].at[c])
            n = levels * extra
            for r in range(len(CHUNKS[c])):
                rows = far_in[:, r * n : (r + 1) * n, :].reshape(places * n, LANES)
                onward[:, r * room : (r + 1) * room, :] = pick(relay_hot[...], rows).reshape(
                    levels, room, LANES
                )

            def pass_on(s, carry):
                level = (my_level + s) % levels
                to = {"gx": gx, "gy": level * low + gy % low}
                remote(
                    onward.at[level],
                    onward_in.at[my_level],
                    sems[4].at[c],
                    sems[5].at[c],
                    to,
                ).start()
                return carry

            lax.fori_loop(1, levels, pass_on, 0)
            onward_in[my_level] = jnp.zeros(onward_in.shape[1:], jnp.float32)
    place_hot[...] = arrival_matrix(plan, known, me, my_level)
    condense(plan, cells_ref, hot, mass, spread, cond)

    for copy in halos:
        copy.wait()
    for k in range(9):
        ext[k, ROW0 - 2 : ROW0, :] = x_recv[0, k]
        ext[k, ROW0 + width : ROW0 + width + 2, :] = x_recv[1, k]
    stencil(plan, ext, mid, coef, cond, fields_out)

    if extra:
        flag = jnp.zeros((devices, 1), jnp.float32)
        totals = [flag] * levels
        owner = lax.broadcasted_iota(jnp.int32, (devices, plan.home_cap), 0)
        for d in range(devices):
            counts = column_sum(jnp.where((lists[d] >> OWN_SHIFT) == owner, 1.0, 0.0))
            level = (d % along) // low
            totals[level] = totals[level] + jnp.maximum(counts - direct, 0.0)
        for total in totals:
            flag = jnp.maximum(flag, jnp.where(total > room, 1.0, 0.0))
        worst = jnp.max(flag, axis=0, keepdims=True)
        flag_out[...] = jnp.broadcast_to(worst, (8, LANES)).astype(jnp.int32)
    else:
        flag_out[...] = jnp.zeros((8, LANES), jnp.int32)

    for c in range(count):
        near_in = buffers[c][1]
        wait_all(near_in, devices - 1, sems[1].at[c])
        if extra:
            far_in, onward_in = buffers[c][3], buffers[c][5]
            wait_all(onward_in, levels - 1, sems[5].at[c])
        for r, attribute in enumerate(CHUNKS[c]):
            parts = [
                near_in[:, r * direct : (r + 1) * direct, :].reshape(devices * direct, LANES)
            ]
            if extra:
                at = pl.multiple_of((r * levels + my_level) * extra, 8)
                parts.append(far_in[:, pl.ds(at, extra), :].reshape(places * extra, LANES))
                parts.append(
                    onward_in[:, r * room : (r + 1) * room, :].reshape(levels * room, LANES)
                )
            if plan.padded > plan.arrivals:
                parts.append(jnp.zeros((plan.padded - plan.arrivals, LANES), jnp.float32))
            rows = jnp.concatenate(parts, axis=0) if len(parts) > 1 else parts[0]
            drops_out[attribute] = pick(place_hot[...], rows)

    wait_all(lists, devices - 1, list_sem.at[0])
    for c in range(count):
        wait_all(buffers[c][0], devices - 1, sems[0].at[c])
        if extra:
            wait_all(buffers[c][2], places - 1, sems[2].at[c])
            wait_all(buffers[c][4], levels - 1, sems[4].at[c])


def run_main(plan, entries, cells, fields, winds, diffusion, planes):
    width, merged, home_cap = plan.width, plan.merged, plan.home_cap
    tall = ROW0 + width + 16
    wide = merged + 2 * LANES
    groups = merged // GROUP
    keys = -(-groups * width // LANES) * LANES
    f32, bf16 = jnp.float32, jnp.bfloat16
    buffers = []
    for chunk in CHUNKS:
        n = len(chunk)
        near = pltpu.VMEM((plan.devices, n * plan.direct, LANES), f32)
        buffers += [near, near]
        if plan.extra:
            far = pltpu.VMEM((plan.places, n * plan.levels * plan.extra, LANES), f32)
            onward = pltpu.VMEM((plan.levels, n * plan.room, LANES), f32)
            buffers += [far, far, onward, onward]
    sem = pltpu.SemaphoreType.DMA((len(CHUNKS),))
    relay_shape = (16, LANES)
    if plan.extra:
        relay_shape = (plan.levels * plan.room, plan.places * plan.levels * plan.extra)
    return pl.pallas_call(
        lambda *refs: main_kernel(plan, *refs),
        out_shape=(
            jax.ShapeDtypeStruct(fields.shape, f32),
            jax.ShapeDtypeStruct((planes.shape[0], OWN_BLK, LANES), f32),
            jax.ShapeDtypeStruct((home_cap, LANES), f32),
            jax.ShapeDtypeStruct((8, LANES), jnp.int32),
        ),
        in_specs=[VMEM, VMEM, ANY, ANY, ANY, ANY],
        out_specs=(VMEM, VMEM, VMEM, VMEM),
        scratch_shapes=[
            pltpu.VMEM((9, tall, wide), f32),
            pltpu.VMEM((5, tall, wide), f32),
            pltpu.VMEM((7, tall, wide), f32),
            pltpu.VMEM((width, merged), f32),
            pltpu.VMEM(planes.shape, f32),
            pltpu.VMEM((plan.devices, 1, home_cap), jnp.int32),
            pltpu.VMEM((plan.slots, home_cap), bf16),
            pltpu.VMEM(relay_shape, bf16),
            pltpu.VMEM((OWN_BLK, plan.padded), bf16),
            pltpu.VMEM((keys, 4 * GROUP), bf16),
            pltpu.VMEM((home_cap, keys), bf16),
            pltpu.VMEM((home_cap, LANES), f32),
            pltpu.VMEM((home_cap, 2 * GROUP), bf16),
            pltpu.VMEM((2, 9, 2, merged), f32),
            pltpu.VMEM((2, 9, 2, wide), f32),
            pltpu.SemaphoreType.DMA((len(LOADS),)),
            pltpu.SemaphoreType.DMA((3,)),
            pltpu.SemaphoreType.DMA((2,)),
            pltpu.SemaphoreType.DMA((8,)),
            pltpu.SemaphoreType.DMA((8,)),
            *buffers,
            *([sem] * (6 if plan.extra else 2)),
        ],
        compiler_params=pltpu.CompilerParams(
            vmem_limit_bytes=LIMIT, collective_id=0, has_side_effects=True
        ),
        cost_estimate=cost(16 << 20, 1 << 28),
        name="condense_advance",
    )(entries, cells, fields, winds, diffusion, planes)


def resend(plan, balance_list, planes, radius):
    everyone = ("gx", "gy")
    devices, cap = plan.devices, plan.cap
    count = planes.shape[0]

    def exchange(x):
        return lax.all_to_all(x, everyone, split_axis=0, concat_axis=0, tiled=True)

    outgoing = pack_drops(
        balance_list.reshape(1, plan.home_cap),
        jnp.concatenate([planes, radius[None]], axis=0),
        devices,
        cap,
    )
    lists = lax.all_gather(balance_list, everyone)
    codes = arrival_codes(lax.axis_index(everyone).reshape(1), lists, cap)
    return place_drops(codes, exchange(outgoing), count)


def per_device(fields, winds, diffusion, droplets, cells, balance_list):
    width = fields.shape[1]
    merged = fields.shape[2]
    home_cap = balance_list.shape[0]
    plan = Plan((lax.axis_size("gx"), lax.axis_size("gy")), home_cap, width, merged)
    planes = droplets.transpose(1, 0, 2)
    fields_out, placed, radius, flag = run_main(
        plan, balance_list.reshape(1, home_cap), cells, fields, winds, diffusion, planes
    )
    if plan.extra:
        placed = lax.cond(
            flag[0, 0] > 0,
            lambda: resend(plan, balance_list, planes, radius),
            lambda: placed,
        )
    return (fields_out, placed.transpose(1, 0, 2))


def solution(mesh):
    return jax.shard_map(
        per_device,
        mesh=mesh,
        in_specs=(
            P(None, "gx", "gy"),
            P(None, "gx", "gy"),
            P("gx", "gy"),
            P(("gx", "gy"), None, None),
            P(("gx", "gy"), None),
            P(("gx", "gy")),
        ),
        out_specs=(P(None, "gx", "gy"), P(("gx", "gy"), None, None)),
        check_vma=False,
    )
```

```python
import math

import jax
import jax.numpy as jnp
from jax import lax
from jax.experimental import pallas as pl
from jax.experimental.pallas import tpu as pltpu
from jax.sharding import PartitionSpec as P

NZ = 48
OWN_BLK = 256
SUBSTEPS = 4
LANES = 128
ROW0 = 16
BATCH = 64
OWN_SHIFT = OWN_BLK.bit_length() - 1
GROUP = math.lcm(NZ, LANES)
SPAN = GROUP // LANES
DIRECT = 8
ROOM = 40
CHUNKS = ((9, 10, 11), (1, 2, 6, 7), (8, 3, 4, 5, 0))
LOADS = ((9, 3), (0, 3), (3, 6))
VMEM = pl.BlockSpec(memory_space=pltpu.VMEM)
SMEM = pl.BlockSpec(memory_space=pltpu.SMEM)
ANY = pl.BlockSpec(memory_space=pl.ANY)
MESH = pl.DeviceIdType.MESH
LIMIT = 56 * 1024 * 1024


def cost(bytes_accessed, flops):
    return pl.CostEstimate(flops=flops, bytes_accessed=bytes_accessed, transcendentals=0)


def split(x):
    high = x.astype(jnp.bfloat16)
    return high, (x - high.astype(jnp.float32)).astype(jnp.bfloat16)


def pick(onehot, x):
    both = jnp.concatenate(split(x), axis=1)
    out = jnp.dot(onehot, both, preferred_element_type=jnp.float32)
    return out[:, :LANES] + out[:, LANES:]


def before_matrix(count):
    row = lax.broadcasted_iota(jnp.int32, (count, count), 0)
    column = lax.broadcasted_iota(jnp.int32, (count, count), 1)
    return jnp.where(row < column, 1.0, 0.0).astype(jnp.bfloat16)


def positions(entries, devices, send_cap):
    home_cap = entries.shape[1]
    owner = jnp.where(entries >= 0, entries >> OWN_SHIFT, devices)
    named = lax.broadcasted_iota(jnp.int32, (devices, home_cap), 0) == owner
    earlier = jnp.dot(
        jnp.where(named, 1.0, 0.0).astype(jnp.bfloat16),
        before_matrix(home_cap),
        preferred_element_type=jnp.float32,
    )
    rank = jnp.sum(jnp.where(named, earlier, 0.0), axis=0, keepdims=True).astype(jnp.int32)
    return jnp.where(entries >= 0, owner * send_cap + rank, devices * send_cap)


def onehot_rows(index, count):
    row = lax.broadcasted_iota(jnp.int32, (count, index.shape[1]), 0)
    return jnp.where(row == index, 1.0, 0.0).astype(jnp.bfloat16)


def pack_kernel(devices, send_cap, entries_ref, drops_ref, moves_ref, out_ref, onehot):
    step = pl.program_id(0)

    @pl.when(step == 0)
    def _():
        position = positions(entries_ref[...], devices, send_cap)
        onehot[...] = onehot_rows(position, devices * send_cap)

    rate = jnp.where((step >= 2) & (step < 5), 0.1, 0.0)
    packed = pick(onehot[...], drops_ref[0] + rate * moves_ref[0])
    out_ref[...] = packed.reshape(devices, send_cap, LANES)


def pack_drops(entries, planes, devices, send_cap):
    count, home_cap, _ = planes.shape
    total = devices * send_cap
    last = count - 1
    return pl.pallas_call(
        lambda *refs: pack_kernel(devices, send_cap, *refs),
        grid=(count - 1,),
        out_shape=jax.ShapeDtypeStruct((devices, (count - 1) * send_cap, LANES), jnp.float32),
        in_specs=[
            pl.BlockSpec((1, home_cap), lambda i: (0, 0)),
            pl.BlockSpec((1, home_cap, LANES), lambda i: (i + 1, 0, 0)),
            pl.BlockSpec((1, home_cap, LANES), lambda i: (jnp.minimum(i + 4, last), 0, 0)),
        ],
        out_specs=pl.BlockSpec((devices, send_cap, LANES), lambda i: (0, i, 0)),
        scratch_shapes=[pltpu.VMEM((total, home_cap), jnp.bfloat16)],
        compiler_params=pltpu.CompilerParams(vmem_limit_bytes=24 * 1024 * 1024),
        cost_estimate=cost(6 << 20, 1 << 20),
        name="pack_drops",
    )(entries, planes, planes)


def codes_kernel(send_cap, me_ref, lists_ref, out_ref):
    homes, home_cap = lists_ref.shape
    entries = lists_ref[...]
    mine = (entries >= 0) & ((entries >> OWN_SHIFT) == me_ref[0])
    earlier = jnp.dot(
        jnp.where(mine, 1.0, 0.0).astype(jnp.bfloat16),
        before_matrix(home_cap),
        preferred_element_type=jnp.float32,
    )
    rank = jnp.where(mine, earlier.astype(jnp.int32), send_cap)
    slot = ((entries & (OWN_BLK - 1)) + 1).astype(jnp.float32)
    lane = lax.broadcasted_iota(jnp.int32, (homes, homes * send_cap), 1)
    home = lax.broadcasted_iota(jnp.int32, (homes, homes * send_cap), 0)
    spread = jnp.zeros((homes, homes * send_cap), jnp.float32)
    for i in range(send_cap):
        code = jnp.sum(jnp.where(rank == i, slot, 0.0), axis=1, keepdims=True)
        spread = jnp.where(lane == home * send_cap + i, code, spread)
    out_ref[...] = jnp.sum(spread, axis=0, keepdims=True).astype(jnp.int32) - 1


def arrival_codes(me, lists, send_cap):
    homes = lists.shape[0]
    return pl.pallas_call(
        lambda *refs: codes_kernel(send_cap, *refs),
        out_shape=jax.ShapeDtypeStruct((1, homes * send_cap), jnp.int32),
        in_specs=[SMEM, VMEM],
        out_specs=VMEM,
        cost_estimate=cost(1 << 18, 1 << 22),
        name="arrival_codes",
    )(me, lists)


def place_kernel(codes_ref, arrived_ref, out_ref, onehot):
    total = codes_ref.shape[1]

    @pl.when(pl.program_id(0) == 0)
    def _():
        onehot[...] = onehot_rows(codes_ref[...], OWN_BLK)

    out_ref[0] = pick(onehot[...], arrived_ref[...].reshape(total, LANES))


def place_drops(codes, arrived, count):
    total = codes.shape[1]
    devices = arrived.shape[0]
    send_cap = total // devices
    return pl.pallas_call(
        place_kernel,
        grid=(count,),
        out_shape=jax.ShapeDtypeStruct((count, OWN_BLK, LANES), jnp.float32),
        in_specs=[
            pl.BlockSpec((1, total), lambda i: (0, 0)),
            pl.BlockSpec((devices, send_cap, LANES), lambda i: (0, (i + count - 1) % count, 0)),
        ],
        out_specs=pl.BlockSpec((1, OWN_BLK, LANES), lambda i: (i, 0, 0)),
        scratch_shapes=[pltpu.VMEM((OWN_BLK, total), jnp.bfloat16)],
        compiler_params=pltpu.CompilerParams(vmem_limit_bytes=16 * 1024 * 1024),
        cost_estimate=cost(5 << 20, 1 << 20),
        name="place_drops",
    )(codes, arrived)

class Plan:
    def __init__(self, axes, home_cap, width, merged):
        self.across, self.along = axes
        self.devices = self.across * self.along
        self.home_cap = home_cap
        self.width, self.merged = width, merged
        self.cap = -(-(home_cap // self.devices) // 8) * 8
        self.direct = min(DIRECT, self.cap)
        self.extra = self.cap - self.direct
        self.low = 2 if self.along % 2 == 0 else 1
        self.levels = self.along // self.low
        self.places = self.across * self.low
        self.room = min(ROOM, self.places * self.extra)
        self.slots = self.devices * self.cap
        arrivals = self.devices * self.direct
        if self.extra:
            arrivals += self.places * self.extra + self.levels * self.room
        self.arrivals = arrivals
        self.padded = -(-arrivals // LANES) * LANES


def quot(v, by):
    return ((v.astype(jnp.float32) + 0.5) * (1.0 / by)).astype(jnp.int32)


def device_parts(plan, d):
    gx = quot(d, plan.along)
    gy = d - gx * plan.along
    level = quot(gy, plan.low)
    place = gx * plan.low + (gy - level * plan.low)
    return level, place


def send_positions(plan, entries):
    home_cap = plan.home_cap
    live = entries >= 0
    owner = jnp.where(live, entries >> OWN_SHIFT, plan.devices)
    named = lax.broadcasted_iota(jnp.int32, (plan.devices, home_cap), 0) == owner
    earlier = jnp.dot(
        jnp.where(named, 1.0, 0.0).astype(jnp.bfloat16),
        before_matrix(home_cap),
        preferred_element_type=jnp.float32,
    )
    rank = jnp.sum(jnp.where(named, earlier, 0.0), axis=0, keepdims=True).astype(jnp.int32)
    position = owner * plan.direct + rank
    if plan.extra:
        level, place = device_parts(plan, owner)
        later = (
            plan.devices * plan.direct
            + (place * plan.levels + level) * plan.extra
            + rank
            - plan.direct
        )
        position = jnp.where(rank < plan.direct, position, later)
    return jnp.where(live, position, plan.slots)


def column_sum(x):
    return jnp.sum(x, axis=1, keepdims=True)


def same_level_before(plan):
    shape = (plan.devices, plan.devices)
    level_r, place_r = device_parts(plan, lax.broadcasted_iota(jnp.int32, shape, 0))
    level_c, place_c = device_parts(plan, lax.broadcasted_iota(jnp.int32, shape, 1))
    return jnp.where((level_r == level_c) & (place_c < place_r), 1.0, 0.0).astype(jnp.bfloat16)


def extra_start(plan, before, over):
    wide = jnp.broadcast_to(over, (plan.devices, LANES)).astype(jnp.bfloat16)
    start = jnp.dot(before, wide, preferred_element_type=jnp.float32)
    return start[:, 0:1]


def arrival_matrix(plan, lists, me, my_level):
    devices, home_cap, direct = plan.devices, plan.home_cap, plan.direct
    mine = (lists >= 0) & ((lists >> OWN_SHIFT) == me)
    flags = jnp.where(mine, 1.0, 0.0)
    earlier = jnp.dot(
        flags.astype(jnp.bfloat16), before_matrix(home_cap), preferred_element_type=jnp.float32
    )
    rank = jnp.where(mine, earlier.astype(jnp.int32), plan.cap)
    slot = ((lists & (OWN_BLK - 1)) + 1).astype(jnp.float32)
    home = lax.broadcasted_iota(jnp.int32, (devices, 1), 0)
    if plan.extra:
        over = jnp.maximum(column_sum(flags) - direct, 0.0)
        start = extra_start(plan, same_level_before(plan), over).astype(jnp.int32)
        level, place = device_parts(plan, home)
    lane = lax.broadcasted_iota(jnp.int32, (devices, plan.padded), 1)
    spread = jnp.zeros((devices, plan.padded), jnp.float32)
    for i in range(plan.cap):
        code = column_sum(jnp.where(rank == i, slot, 0.0))
        if i < direct:
            at = home * direct + i
        else:
            near = devices * direct + place * plan.extra + i - direct
            within = start + i - direct
            far = devices * direct + plan.places * plan.extra + level * plan.room + within
            far = jnp.where(within < plan.room, far, plan.padded)
            at = jnp.where(level == my_level, near, far)
        spread = jnp.where((lane == at) & (code > 0.0), code, spread)
    row = jnp.sum(spread, axis=0, keepdims=True).astype(jnp.int32) - 1
    return onehot_rows(row, OWN_BLK)


def relay_matrix(plan, lists, my_level, my_place):
    devices, levels, extra, room = plan.devices, plan.levels, plan.extra, plan.room
    before = same_level_before(plan)
    columns = plan.places * levels * extra
    lane = lax.broadcasted_iota(jnp.int32, (devices, columns), 1)
    lane_place = quot(lane, levels * extra)
    lane_level = quot(lane - lane_place * (levels * extra), extra)
    lane_item = lane - (lane_place * levels + lane_level) * extra
    home = lax.broadcasted_iota(jnp.int32, (devices, 1), 0)
    home_level, home_place = device_parts(plan, home)
    place_gx = my_place // plan.low
    place_gy = my_place % plan.low
    spread = jnp.zeros((devices, columns), jnp.float32)
    for level in range(levels):
        owner = place_gx * plan.along + level * plan.low + place_gy
        named = (lists >= 0) & ((lists >> OWN_SHIFT) == owner)
        over = jnp.maximum(column_sum(jnp.where(named, 1.0, 0.0)) - plan.direct, 0.0)
        start = extra_start(plan, before, over)
        within = start + lane_item.astype(jnp.float32)
        ok = (
            (home_level == my_level)
            & (home_place == lane_place)
            & (lane_level == level)
            & (lane_item.astype(jnp.float32) < over)
            & (within < room)
        )
        spread = jnp.where(ok, within + (level * room + 1), spread)
    row = jnp.sum(spread, axis=0, keepdims=True).astype(jnp.int32) - 1
    return onehot_rows(row, levels * room)


def faces(c_low, c_high, k_low, k_high):
    courant = 0.5 * (c_low + c_high)
    diffuse = 0.5 * (k_low + k_high)
    return jnp.maximum(courant, 0.0) + diffuse, jnp.minimum(courant, 0.0) - diffuse


def stencil(plan, ext, mid, coef, cond_ref, out_ref):
    width, merged = plan.width, plan.merged
    lanes = merged + 2 * LANES
    core = slice(LANES, LANES + merged)
    chunks = range(ROW0 - 8, ROW0 + width + 8, 8)
    z = (lax.broadcasted_iota(jnp.int32, (8, lanes), 1) + (NZ - LANES % NZ)) % NZ
    top = z == NZ - 1
    bottom = z == 0

    def ahead(v, n):
        return pltpu.roll(v, lanes - n, 1)

    def behind(v, n):
        return pltpu.roll(v, n, 1)

    def coefficients():
        for base in chunks:
            rows = slice(base, base + 8)
            up = slice(base + 1, base + 9)
            down = slice(base - 1, base + 7)
            k0 = ext[8, rows, :]
            u0 = ext[5, rows, :]
            p, n = faces(u0, ext[5, up, :], k0, ext[8, up, :])
            p_low, n_low = faces(ext[5, down, :], u0, ext[8, down, :], k0)
            centre = 1.0 - (p - n_low)
            coef[0, rows, :] = -n
            coef[1, rows, :] = p_low
            v0 = ext[6, rows, :]
            p, n = faces(v0, ahead(v0, NZ), k0, ahead(k0, NZ))
            centre = centre - (p - behind(n, NZ))
            coef[2, rows, :] = -n
            coef[3, rows, :] = behind(p, NZ)
            w0 = ext[7, rows, :]
            p, n = faces(w0, ahead(w0, 1), k0, ahead(k0, 1))
            p = jnp.where(top, 0.0, p)
            n = jnp.where(top, 0.0, n)
            coef[4, rows, :] = -n
            p_low = jnp.where(bottom, 0.0, behind(p, 1))
            n_low = jnp.where(bottom, 0.0, behind(n, 1))
            coef[5, rows, :] = p_low
            coef[6, rows, :] = centre - (p - n_low)

    def update(src, f, base):
        rows = slice(base, base + 8)
        mine = src[f, rows, :]
        new = coef[6, rows, :] * mine
        new += coef[0, rows, :] * src[f, base + 1 : base + 9, :]
        new += coef[1, rows, :] * src[f, base - 1 : base + 7, :]
        new += coef[2, rows, :] * ahead(mine, NZ)
        new += coef[3, rows, :] * behind(mine, NZ)
        new += coef[4, rows, :] * ahead(mine, 1)
        new += coef[5, rows, :] * behind(mine, 1)
        return new

    def first(f, carry):
        for base in chunks:
            mid[f, base : base + 8, :] = update(ext, f, base)
        return carry

    def advance_once():
        lax.fori_loop(0, 5, first, 0)

    def second(f, carry):
        share = jnp.where(f == 0, 0.25, jnp.where(f == 1, -0.1, 0.0))
        for base in range(ROW0, ROW0 + width, 8):
            at = slice(base - ROW0, base - ROW0 + 8)
            out_ref[f, at, :] = update(mid, f, base)[:, core] + share * cond_ref[at, :]
        return carry

    def advance_twice():
        lax.fori_loop(0, 5, second, 0)

    return coefficients, advance_once, advance_twice


def grow_drops(plan, entries_ref, cells_ref, ext, drops, tab, hot, radius_out, mass):
    width = plan.width
    groups = plan.merged // GROUP
    used = groups * width
    for f in range(2):
        for g in range(groups):
            lanes = slice(LANES + g * GROUP, LANES + (g + 1) * GROUP)
            high, low = split(ext[f, ROW0 : ROW0 + width, lanes])
            tab[g * width : (g + 1) * width, 2 * f * GROUP : (2 * f + 1) * GROUP] = high
            tab[g * width : (g + 1) * width, (2 * f + 1) * GROUP : (2 * f + 2) * GROUP] = low
    if tab.shape[0] > used:
        tab[used:, :] = jnp.zeros((tab.shape[0] - used, tab.shape[1]), jnp.bfloat16)
    live_count = jnp.sum(
        jnp.where(entries_ref[...] >= 0, 1.0, 0.0), axis=1, keepdims=True
    ).astype(jnp.int32)

    def in_group(rows):
        c = cells_ref[rows, :]
        return c, quot(c[:, 0:1], GROUP)

    def one(g, carry):
        at = pl.multiple_of(g * BATCH, BATCH)
        rows = pl.ds(at, BATCH)
        c, q = in_group(rows)
        x = quot(q, groups)
        key = (q - x * groups) * width + x
        lane = lax.broadcasted_iota(jnp.int32, (BATCH, hot.shape[1]), 1)
        chosen = jnp.where(lane == key, 1.0, 0.0).astype(jnp.bfloat16)
        hot[rows, :] = chosen
        both = jnp.dot(chosen, tab[...], preferred_element_type=jnp.float32)
        offset = c - q * GROUP
        part = offset >> 7
        within = offset & (LANES - 1)

        def look(f):
            high = both[:, 2 * f * GROUP : (2 * f + 1) * GROUP]
            value = high + both[:, (2 * f + 1) * GROUP : (2 * f + 2) * GROUP]
            got = jnp.take_along_axis(value[:, :LANES], within, axis=1)
            for t in range(1, SPAN):
                tile = value[:, t * LANES : (t + 1) * LANES]
                got = jnp.where(part == t, jnp.take_along_axis(tile, within, axis=1), got)
            return got

        theta, vapour = look(0), look(1)
        supersat = vapour - 0.5 * jnp.tanh(theta)
        growth_rate = 1.0 / (1.0 + 0.1 * theta * theta)
        start = drops[0, rows, :]
        solute = drops[1, rows, :]
        weight = drops[2, rows, :]
        square = start * start
        for _ in range(SUBSTEPS):
            radius = jnp.sqrt(square)
            square = jnp.maximum(
                square
                + 0.05
                * growth_rate
                * (supersat - 0.02 / radius + solute / (radius * radius * radius)),
                0.04,
            )
        radius = jnp.sqrt(square)
        radius_out[rows, :] = radius
        grown = weight * (radius * square - start * start * start)
        block = at + lax.broadcasted_iota(jnp.int32, (BATCH, LANES), 0)
        mass[rows, :] = jnp.where(block < live_count, grown, 0.0)
        return carry

    lax.fori_loop(0, plan.home_cap // BATCH, one, 0)


def condense(plan, cells_ref, hot, mass, spread, cond):
    width = plan.width
    groups = plan.merged // GROUP
    row = lax.broadcasted_iota(jnp.int32, (LANES, LANES), 0)
    column = lax.broadcasted_iota(jnp.int32, (LANES, LANES), 1)
    upper = (row <= column).astype(jnp.float32)
    mass[...] = jnp.dot(
        mass[...], upper, precision=lax.Precision.HIGHEST, preferred_element_type=jnp.float32
    )
    lane = lax.broadcasted_iota(jnp.int32, (BATCH, LANES), 1)

    def sums(g, carry):
        rows = pl.ds(pl.multiple_of(g * BATCH, BATCH), BATCH)
        c = cells_ref[rows, :]
        offset = c - quot(c[:, 0:1], GROUP) * GROUP
        column = quot(offset[:, 0:1], NZ)
        level = offset - column * NZ
        count = jnp.zeros((BATCH, LANES), jnp.int32)
        step = LANES
        while step >= 1:
            probe = jnp.minimum(count + (step - 1), LANES - 1)
            below = jnp.take_along_axis(level, probe, axis=1) <= lane
            count = jnp.where(below & (count + step <= LANES), count + step, count)
            step //= 2
        upto = jnp.take_along_axis(mass[rows, :], jnp.maximum(count - 1, 0), axis=1)
        upto = jnp.where(count > 0, upto, 0.0)
        before = jnp.where(lane == 0, 0.0, pltpu.roll(upto, 1, 1))
        picked = upto - before
        for t in range(SPAN):
            place = lane + t * LANES
            which = quot(place, NZ)
            here = jnp.take_along_axis(picked, place - which * NZ, axis=1)
            high, low = split(jnp.where(which == column, here, 0.0))
            spread[rows, t * LANES : (t + 1) * LANES] = high
            spread[rows, GROUP + t * LANES : GROUP + (t + 1) * LANES] = low
        return carry

    lax.fori_loop(0, plan.home_cap // BATCH, sums, 0)
    both = lax.dot_general(
        hot[...], spread[...], (((0,), (0,)), ((), ())), preferred_element_type=jnp.float32
    )
    for g in range(groups):
        rows = slice(g * width, (g + 1) * width)
        cond[:, g * GROUP : (g + 1) * GROUP] = both[rows, :GROUP] + both[rows, GROUP:]


def main_kernel(
    plan,
    entries_ref,
    cells_ref,
    fields_hbm,
    winds_hbm,
    diff_hbm,
    planes_hbm,
    fields_hbm_out,
    drops_hbm_out,
    radius_out,
    flag_out,
    fields_out,
    drops_out,
    out_sem,
    ext,
    mid,
    coef,
    cond,
    drops,
    lists,
    pack_hot,
    relay_hot,
    place_hot,
    tab,
    hot,
    mass,
    spread,
    x_send,
    x_recv,
    load_sem,
    grid_sem,
    list_sem,
    halo_send,
    halo_recv,
    *chunk_refs,
):
    devices, across, along = plan.devices, plan.across, plan.along
    low, levels, places = plan.low, plan.levels, plan.places
    direct, extra, room = plan.direct, plan.extra, plan.room
    width, merged = plan.width, plan.merged
    count = len(CHUNKS)
    per = 6 if extra else 2
    buffers = [chunk_refs[i * per : (i + 1) * per] for i in range(count)]
    sems = chunk_refs[count * per :]
    gx = lax.axis_index("gx")
    gy = lax.axis_index("gy")
    me = gx * along + gy
    my_level = gy // low
    my_place = gx * low + gy % low
    barrier = pltpu.get_barrier_semaphore()

    def device(d):
        return {"gx": d // along, "gy": d % along}

    def greet(s, carry):
        other = (me + s) % devices
        pl.semaphore_signal(barrier, inc=1, device_id=device(other), device_id_type=MESH)
        return carry

    lax.fori_loop(1, devices, greet, 0)

    loads = []
    for i, (at, n) in enumerate(LOADS):
        rows = pl.ds(at, n)
        loads.append(pltpu.make_async_copy(planes_hbm.at[rows], drops.at[rows], load_sem.at[i]))
    own_rows = pl.ds(ROW0, width)
    own_lanes = pl.ds(LANES, merged)
    grids = (
        pltpu.make_async_copy(
            fields_hbm, ext.at[pl.ds(0, 5), own_rows, own_lanes], grid_sem.at[0]
        ),
        pltpu.make_async_copy(winds_hbm, ext.at[pl.ds(5, 3), own_rows, own_lanes], grid_sem.at[1]),
        pltpu.make_async_copy(diff_hbm, ext.at[8, own_rows, own_lanes], grid_sem.at[2]),
    )
    loads[0].start()
    for grid in grids:
        grid.start()
    loads[1].start()
    loads[2].start()

    pack_hot[...] = onehot_rows(send_positions(plan, entries_ref[...]), plan.slots)
    pl.semaphore_wait(barrier, devices - 1)

    def remote(src, dst, send_sem, recv_sem, to):
        return pltpu.make_async_remote_copy(
            src_ref=src,
            dst_ref=dst,
            send_sem=send_sem,
            recv_sem=recv_sem,
            device_id=to,
            device_id_type=MESH,
        )

    halos = []

    def halo(src, dst, dx, dy):
        i = len(halos)
        to = {"gx": (gx + dx + across) % across, "gy": (gy + dy + along) % along}
        copy = remote(src, dst, halo_send.at[i], halo_recv.at[i], to)
        copy.start()
        halos.append(copy)

    left_lanes = pl.ds(0, LANES)
    right_lanes = pl.ds(LANES + merged, LANES)
    begin, end = pl.ds(0, LANES), pl.ds(merged - LANES, LANES)

    def y_halos():
        for lanes, to_lanes, dy in ((begin, right_lanes, -1), (end, left_lanes, 1)):
            halo(
                fields_hbm.at[pl.ds(0, 5), pl.ds(0, width), lanes],
                ext.at[pl.ds(0, 5), own_rows, to_lanes],
                0,
                dy,
            )
            halo(
                winds_hbm.at[pl.ds(0, 3), pl.ds(0, width), lanes],
                ext.at[pl.ds(5, 3), own_rows, to_lanes],
                0,
                dy,
            )
            halo(diff_hbm.at[pl.ds(0, width), lanes], ext.at[8, own_rows, to_lanes], 0, dy)

    def x_halos():
        for grid in grids:
            grid.wait()
        for k in range(9):
            x_send[0, k] = ext[k, ROW0 : ROW0 + 2, LANES : LANES + merged]
            x_send[1, k] = ext[k, ROW0 + width - 2 : ROW0 + width, LANES : LANES + merged]
        every, both = pl.ds(0, 9), pl.ds(0, 2)
        for side, dx in ((0, -1), (1, 1)):
            to = x_recv.at[1 - side]
            halo(x_send.at[side], to.at[every, both, own_lanes], dx, 0)
            halo(x_send.at[side, every, both, begin], to.at[every, both, right_lanes], dx, -1)
            halo(x_send.at[side, every, both, end], to.at[every, both, left_lanes], dx, 1)

    def tell(s, carry):
        other = (me + s) % devices
        remote(entries_ref, lists.at[me], list_sem.at[0], list_sem.at[1], device(other)).start()
        return carry

    def pack(c):
        near, far = buffers[c][0], buffers[c][2] if extra else None
        for r, attribute in enumerate(CHUNKS[c]):
            if attribute == 0:
                value = radius_out[...]
            else:
                value = drops[attribute]
                if 3 <= attribute < 6:
                    value = value + 0.1 * drops[attribute + 3]
            packed = pick(pack_hot[...], value)
            cut = devices * direct
            near[:, r * direct : (r + 1) * direct, :] = packed[:cut].reshape(
                devices, direct, LANES
            )
            if extra:
                n = levels * extra
                far[:, r * n : (r + 1) * n, :] = packed[cut:].reshape(places, n, LANES)

    def send(c):
        near, near_in = buffers[c][0:2]
        if extra:
            far, far_in = buffers[c][2:4]

            def give(s, carry):
                place = (my_place + s) % places
                to = {"gx": place // low, "gy": my_level * low + place % low}
                remote(
                    far.at[place], far_in.at[my_place], sems[2].at[c], sems[3].at[c], to
                ).start()
                return carry

            lax.fori_loop(1, places, give, 0)
            far_in[my_place] = far[my_place]

        def out(s, carry):
            other = (me + s) % devices
            remote(
                near.at[other], near_in.at[me], sems[0].at[c], sems[1].at[c], device(other)
            ).start()
            return carry

        lax.fori_loop(1, devices, out, 0)
        near_in[me] = near[me]

    def wait_all(ref, n, sem):
        part = ref.at[pl.ds(0, n)]
        pltpu.make_async_copy(part, part, sem).wait()

    def relay(c):
        far_in, onward, onward_in = buffers[c][3:6]
        wait_all(far_in, places - 1, sems[3].at[c])
        n = levels * extra
        for r in range(len(CHUNKS[c])):
            rows = far_in[:, r * n : (r + 1) * n, :].reshape(places * n, LANES)
            onward[:, r * room : (r + 1) * room, :] = pick(relay_hot[...], rows).reshape(
                levels, room, LANES
            )

        def pass_on(s, carry):
            level = (my_level + s) % levels
            to = {"gx": gx, "gy": level * low + gy % low}
            remote(
                onward.at[level], onward_in.at[my_level], sems[4].at[c], sems[5].at[c], to
            ).start()
            return carry

        lax.fori_loop(1, levels, pass_on, 0)
        onward_in[my_level] = jnp.zeros(onward_in.shape[1:], jnp.float32)

    loads[0].wait()
    pack(0)
    send(0)
    y_halos()
    x_halos()
    lax.fori_loop(1, devices, tell, 0)
    loads[1].wait()
    loads[2].wait()
    pack(1)
    send(1)
    grow_drops(plan, entries_ref, cells_ref, ext, drops, tab, hot, radius_out, mass)
    pack(2)
    send(2)
    condense(plan, cells_ref, hot, mass, spread, cond)

    for copy in halos:
        copy.wait()
    for k in range(9):
        ext[k, ROW0 - 2 : ROW0, :] = x_recv[0, k]
        ext[k, ROW0 + width : ROW0 + width + 2, :] = x_recv[1, k]
    coefficients, advance_once, advance_twice = stencil(plan, ext, mid, coef, cond, fields_out)
    coefficients()

    wait_all(lists, devices - 1, list_sem.at[1])
    lists[me] = entries_ref[...]
    known = jnp.concatenate([lists[d] for d in range(devices)], axis=0)
    if extra:
        relay_hot[...] = relay_matrix(plan, known, my_level, my_place)
        relay(0)
        relay(1)
    advance_once()
    if extra:
        relay(2)
    place_hot[...] = arrival_matrix(plan, known, me, my_level)
    advance_twice()
    finished = []

    def finish(which, src, dst, i):
        copy = pltpu.make_async_copy(src.at[i], dst.at[i], out_sem.at[which, i])
        copy.start()
        finished.append(copy)

    for f in range(5):
        finish(0, fields_out, fields_hbm_out, f)

    if extra:
        flag = jnp.zeros((devices, 1), jnp.float32)
        totals = [flag] * levels
        owner = lax.broadcasted_iota(jnp.int32, (devices, plan.home_cap), 0)
        for d in range(devices):
            counts = column_sum(jnp.where((lists[d] >> OWN_SHIFT) == owner, 1.0, 0.0))
            level = (d % along) // low
            totals[level] = totals[level] + jnp.maximum(counts - direct, 0.0)
        for total in totals:
            flag = jnp.maximum(flag, jnp.where(total > room, 1.0, 0.0))
        flag_out[0] = jnp.max(flag).astype(jnp.int32)
    else:
        flag_out[0] = 0

    for c in range(count):
        near_in = buffers[c][1]
        wait_all(near_in, devices - 1, sems[1].at[c])
        if extra:
            far_in, onward_in = buffers[c][3], buffers[c][5]
            wait_all(onward_in, levels - 1, sems[5].at[c])
        for r, attribute in enumerate(CHUNKS[c]):
            parts = [
                near_in[:, r * direct : (r + 1) * direct, :].reshape(devices * direct, LANES)
            ]
            if extra:
                at = pl.multiple_of((r * levels + my_level) * extra, 8)
                parts.append(far_in[:, pl.ds(at, extra), :].reshape(places * extra, LANES))
                parts.append(
                    onward_in[:, r * room : (r + 1) * room, :].reshape(levels * room, LANES)
                )
            if plan.padded > plan.arrivals:
                parts.append(jnp.zeros((plan.padded - plan.arrivals, LANES), jnp.float32))
            rows = jnp.concatenate(parts, axis=0) if len(parts) > 1 else parts[0]
            drops_out[attribute] = pick(place_hot[...], rows)
            finish(1, drops_out, drops_hbm_out, attribute)

    for copy in finished:
        copy.wait()
    wait_all(lists, devices - 1, list_sem.at[0])
    for c in range(count):
        wait_all(buffers[c][0], devices - 1, sems[0].at[c])
        if extra:
            wait_all(buffers[c][2], places - 1, sems[2].at[c])
            wait_all(buffers[c][4], levels - 1, sems[4].at[c])


def run_main(plan, entries, cells, fields, winds, diffusion, planes):
    width, merged, home_cap = plan.width, plan.merged, plan.home_cap
    tall = ROW0 + width + 16
    wide = merged + 2 * LANES
    groups = merged // GROUP
    keys = -(-groups * width // LANES) * LANES
    f32, bf16 = jnp.float32, jnp.bfloat16
    buffers = []
    for chunk in CHUNKS:
        n = len(chunk)
        near = pltpu.VMEM((plan.devices, n * plan.direct, LANES), f32)
        buffers += [near, near]
        if plan.extra:
            far = pltpu.VMEM((plan.places, n * plan.levels * plan.extra, LANES), f32)
            onward = pltpu.VMEM((plan.levels, n * plan.room, LANES), f32)
            buffers += [far, far, onward, onward]
    sem = pltpu.SemaphoreType.DMA((len(CHUNKS),))
    relay_shape = (16, LANES)
    if plan.extra:
        relay_shape = (plan.levels * plan.room, plan.places * plan.levels * plan.extra)
    return pl.pallas_call(
        lambda *refs: main_kernel(plan, *refs),
        out_shape=(
            jax.ShapeDtypeStruct(fields.shape, f32),
            jax.ShapeDtypeStruct((planes.shape[0], OWN_BLK, LANES), f32),
            jax.ShapeDtypeStruct((home_cap, LANES), f32),
            jax.ShapeDtypeStruct((1,), jnp.int32),
        ),
        in_specs=[VMEM, VMEM, ANY, ANY, ANY, ANY],
        out_specs=(ANY, ANY, VMEM, SMEM),
        scratch_shapes=[
            pltpu.VMEM(fields.shape, f32),
            pltpu.VMEM((planes.shape[0], OWN_BLK, LANES), f32),
            pltpu.SemaphoreType.DMA((2, max(planes.shape[0], fields.shape[0]))),
            pltpu.VMEM((9, tall, wide), f32),
            pltpu.VMEM((5, tall, wide), f32),
            pltpu.VMEM((7, tall, wide), f32),
            pltpu.VMEM((width, merged), f32),
            pltpu.VMEM(planes.shape, f32),
            pltpu.VMEM((plan.devices, 1, home_cap), jnp.int32),
            pltpu.VMEM((plan.slots, home_cap), bf16),
            pltpu.VMEM(relay_shape, bf16),
            pltpu.VMEM((OWN_BLK, plan.padded), bf16),
            pltpu.VMEM((keys, 4 * GROUP), bf16),
            pltpu.VMEM((home_cap, keys), bf16),
            pltpu.VMEM((home_cap, LANES), f32),
            pltpu.VMEM((home_cap, 2 * GROUP), bf16),
            pltpu.VMEM((2, 9, 2, merged), f32),
            pltpu.VMEM((2, 9, 2, wide), f32),
            pltpu.SemaphoreType.DMA((len(LOADS),)),
            pltpu.SemaphoreType.DMA((3,)),
            pltpu.SemaphoreType.DMA((2,)),
            pltpu.SemaphoreType.DMA((12,)),
            pltpu.SemaphoreType.DMA((12,)),
            *buffers,
            *([sem] * (6 if plan.extra else 2)),
        ],
        compiler_params=pltpu.CompilerParams(
            vmem_limit_bytes=LIMIT, collective_id=0, has_side_effects=True
        ),
        cost_estimate=cost(16 << 20, 1 << 28),
        name="condense_advance",
    )(entries, cells, fields, winds, diffusion, planes)


def hand_kernel(fields_ref, drops_ref, fields_out, drops_out, fields_held, drops_held, sem):
    arrays = ((fields_ref, fields_held, fields_out), (drops_ref, drops_held, drops_out))
    pieces = [(a, i) for a in arrays for i in range(a[0].shape[0])]

    def move(n, step):
        refs, i = pieces[n]
        return pltpu.make_async_copy(refs[step].at[i], refs[step + 1].at[i], sem.at[step, n])

    for n in range(len(pieces)):
        move(n, 0).start()
    for n in range(len(pieces)):
        move(n, 0).wait()
        move(n, 1).start()
    for n in range(len(pieces)):
        move(n, 1).wait()


def hand_over(fields, drops):
    return pl.pallas_call(
        hand_kernel,
        out_shape=(
            jax.ShapeDtypeStruct(fields.shape, jnp.float32),
            jax.ShapeDtypeStruct(drops.shape, jnp.float32),
        ),
        in_specs=[ANY, ANY],
        out_specs=(ANY, ANY),
        scratch_shapes=[
            pltpu.VMEM(fields.shape, jnp.float32),
            pltpu.VMEM(drops.shape, jnp.float32),
            pltpu.SemaphoreType.DMA((2, fields.shape[0] + drops.shape[0])),
        ],
        compiler_params=pltpu.CompilerParams(vmem_limit_bytes=LIMIT),
        cost_estimate=cost(8 << 20, 1 << 10),
        name="hand_over",
    )(fields, drops)


def resend(plan, balance_list, planes, radius):
    everyone = ("gx", "gy")
    devices, cap = plan.devices, plan.cap
    count = planes.shape[0]

    def exchange(x):
        return lax.all_to_all(x, everyone, split_axis=0, concat_axis=0, tiled=True)

    outgoing = pack_drops(
        balance_list.reshape(1, plan.home_cap),
        jnp.concatenate([planes, radius[None]], axis=0),
        devices,
        cap,
    )
    lists = lax.all_gather(balance_list, everyone)
    codes = arrival_codes(lax.axis_index(everyone).reshape(1), lists, cap)
    return place_drops(codes, exchange(outgoing), count)


def per_device(fields, winds, diffusion, droplets, cells, balance_list):
    width = fields.shape[1]
    merged = fields.shape[2]
    home_cap = balance_list.shape[0]
    plan = Plan((lax.axis_size("gx"), lax.axis_size("gy")), home_cap, width, merged)
    planes = droplets.transpose(1, 0, 2)
    fields_out, placed, radius, flag = run_main(
        plan, balance_list.reshape(1, home_cap), cells, fields, winds, diffusion, planes
    )
    fields_out, placed = hand_over(fields_out, placed)
    if plan.extra:
        placed = lax.cond(
            flag[0] > 0,
            lambda: resend(plan, balance_list, planes, radius),
            lambda: placed,
        )
    return (fields_out, placed.transpose(1, 0, 2))


def solution(mesh):
    return jax.shard_map(
        per_device,
        mesh=mesh,
        in_specs=(
            P(None, "gx", "gy"),
            P(None, "gx", "gy"),
            P("gx", "gy"),
            P(("gx", "gy"), None, None),
            P(("gx", "gy"), None),
            P(("gx", "gy")),
        ),
        out_specs=(P(None, "gx", "gy"), P(("gx", "gy"), None, None)),
        check_vma=False,
    )
```

```python
import math

import jax
import jax.numpy as jnp
from jax import lax
from jax.experimental import pallas as pl
from jax.experimental.pallas import tpu as pltpu
from jax.sharding import PartitionSpec as P

NZ = 48
OWN_BLK = 256
SUBSTEPS = 4
LANES = 128
ROW0 = 16
BATCH = 64
OWN_SHIFT = OWN_BLK.bit_length() - 1
GROUP = math.lcm(NZ, LANES)
SPAN = GROUP // LANES
DIRECT = 8
ROOM = 40
CHUNKS = ((9, 10, 11), (1, 2, 6, 7), (8, 3, 4, 5, 0))
LOADS = ((9, 3), (0, 3), (3, 6))
Y_EDGE = ((0, 2), (1, 2), (2, 2), (3, 2), (4, 2), (6, 2), (8, 2), (5, 1), (7, 1))
VMEM = pl.BlockSpec(memory_space=pltpu.VMEM)
SMEM = pl.BlockSpec(memory_space=pltpu.SMEM)
ANY = pl.BlockSpec(memory_space=pl.ANY)
MESH = pl.DeviceIdType.MESH
LIMIT = 56 * 1024 * 1024


def cost(bytes_accessed, flops):
    return pl.CostEstimate(flops=flops, bytes_accessed=bytes_accessed, transcendentals=0)


def split(x):
    high = x.astype(jnp.bfloat16)
    return high, (x - high.astype(jnp.float32)).astype(jnp.bfloat16)


def pick(onehot, x):
    both = jnp.concatenate(split(x), axis=1)
    out = jnp.dot(onehot, both, preferred_element_type=jnp.float32)
    return out[:, :LANES] + out[:, LANES:]


def before_matrix(count):
    row = lax.broadcasted_iota(jnp.int32, (count, count), 0)
    column = lax.broadcasted_iota(jnp.int32, (count, count), 1)
    return jnp.where(row < column, 1.0, 0.0).astype(jnp.bfloat16)


def positions(entries, devices, send_cap):
    home_cap = entries.shape[1]
    owner = jnp.where(entries >= 0, entries >> OWN_SHIFT, devices)
    named = lax.broadcasted_iota(jnp.int32, (devices, home_cap), 0) == owner
    earlier = jnp.dot(
        jnp.where(named, 1.0, 0.0).astype(jnp.bfloat16),
        before_matrix(home_cap),
        preferred_element_type=jnp.float32,
    )
    rank = jnp.sum(jnp.where(named, earlier, 0.0), axis=0, keepdims=True).astype(jnp.int32)
    return jnp.where(entries >= 0, owner * send_cap + rank, devices * send_cap)


def onehot_rows(index, count):
    row = lax.broadcasted_iota(jnp.int32, (count, index.shape[1]), 0)
    return jnp.where(row == index, 1.0, 0.0).astype(jnp.bfloat16)


def pack_kernel(devices, send_cap, entries_ref, drops_ref, moves_ref, out_ref, onehot):
    step = pl.program_id(0)

    @pl.when(step == 0)
    def _():
        position = positions(entries_ref[...], devices, send_cap)
        onehot[...] = onehot_rows(position, devices * send_cap)

    rate = jnp.where((step >= 2) & (step < 5), 0.1, 0.0)
    packed = pick(onehot[...], drops_ref[0] + rate * moves_ref[0])
    out_ref[...] = packed.reshape(devices, send_cap, LANES)


def pack_drops(entries, planes, devices, send_cap):
    count, home_cap, _ = planes.shape
    total = devices * send_cap
    last = count - 1
    return pl.pallas_call(
        lambda *refs: pack_kernel(devices, send_cap, *refs),
        grid=(count - 1,),
        out_shape=jax.ShapeDtypeStruct((devices, (count - 1) * send_cap, LANES), jnp.float32),
        in_specs=[
            pl.BlockSpec((1, home_cap), lambda i: (0, 0)),
            pl.BlockSpec((1, home_cap, LANES), lambda i: (i + 1, 0, 0)),
            pl.BlockSpec((1, home_cap, LANES), lambda i: (jnp.minimum(i + 4, last), 0, 0)),
        ],
        out_specs=pl.BlockSpec((devices, send_cap, LANES), lambda i: (0, i, 0)),
        scratch_shapes=[pltpu.VMEM((total, home_cap), jnp.bfloat16)],
        compiler_params=pltpu.CompilerParams(vmem_limit_bytes=24 * 1024 * 1024),
        cost_estimate=cost(6 << 20, 1 << 20),
        name="pack_drops",
    )(entries, planes, planes)


def codes_kernel(send_cap, me_ref, lists_ref, out_ref):
    homes, home_cap = lists_ref.shape
    entries = lists_ref[...]
    mine = (entries >= 0) & ((entries >> OWN_SHIFT) == me_ref[0])
    earlier = jnp.dot(
        jnp.where(mine, 1.0, 0.0).astype(jnp.bfloat16),
        before_matrix(home_cap),
        preferred_element_type=jnp.float32,
    )
    rank = jnp.where(mine, earlier.astype(jnp.int32), send_cap)
    slot = ((entries & (OWN_BLK - 1)) + 1).astype(jnp.float32)
    lane = lax.broadcasted_iota(jnp.int32, (homes, homes * send_cap), 1)
    home = lax.broadcasted_iota(jnp.int32, (homes, homes * send_cap), 0)
    spread = jnp.zeros((homes, homes * send_cap), jnp.float32)
    for i in range(send_cap):
        code = jnp.sum(jnp.where(rank == i, slot, 0.0), axis=1, keepdims=True)
        spread = jnp.where(lane == home * send_cap + i, code, spread)
    out_ref[...] = jnp.sum(spread, axis=0, keepdims=True).astype(jnp.int32) - 1


def arrival_codes(me, lists, send_cap):
    homes = lists.shape[0]
    return pl.pallas_call(
        lambda *refs: codes_kernel(send_cap, *refs),
        out_shape=jax.ShapeDtypeStruct((1, homes * send_cap), jnp.int32),
        in_specs=[SMEM, VMEM],
        out_specs=VMEM,
        cost_estimate=cost(1 << 18, 1 << 22),
        name="arrival_codes",
    )(me, lists)


def place_kernel(codes_ref, arrived_ref, out_ref, onehot):
    total = codes_ref.shape[1]

    @pl.when(pl.program_id(0) == 0)
    def _():
        onehot[...] = onehot_rows(codes_ref[...], OWN_BLK)

    out_ref[0] = pick(onehot[...], arrived_ref[...].reshape(total, LANES))


def place_drops(codes, arrived, count):
    total = codes.shape[1]
    devices = arrived.shape[0]
    send_cap = total // devices
    return pl.pallas_call(
        place_kernel,
        grid=(count,),
        out_shape=jax.ShapeDtypeStruct((count, OWN_BLK, LANES), jnp.float32),
        in_specs=[
            pl.BlockSpec((1, total), lambda i: (0, 0)),
            pl.BlockSpec((devices, send_cap, LANES), lambda i: (0, (i + count - 1) % count, 0)),
        ],
        out_specs=pl.BlockSpec((1, OWN_BLK, LANES), lambda i: (i, 0, 0)),
        scratch_shapes=[pltpu.VMEM((OWN_BLK, total), jnp.bfloat16)],
        compiler_params=pltpu.CompilerParams(vmem_limit_bytes=16 * 1024 * 1024),
        cost_estimate=cost(5 << 20, 1 << 20),
        name="place_drops",
    )(codes, arrived)

class Plan:
    def __init__(self, axes, home_cap, width, merged):
        self.across, self.along = axes
        self.devices = self.across * self.along
        self.home_cap = home_cap
        self.width, self.merged = width, merged
        self.cap = -(-(home_cap // self.devices) // 8) * 8
        self.direct = min(DIRECT, self.cap)
        self.extra = self.cap - self.direct
        self.low = 2 if self.along % 2 == 0 else 1
        self.levels = self.along // self.low
        self.places = self.across * self.low
        self.room = min(ROOM, self.places * self.extra)
        self.slots = self.devices * self.cap
        arrivals = self.devices * self.direct
        if self.extra:
            arrivals += self.places * self.extra + self.levels * self.room
        self.arrivals = arrivals
        self.padded = -(-arrivals // LANES) * LANES


def quot(v, by):
    return ((v.astype(jnp.float32) + 0.5) * (1.0 / by)).astype(jnp.int32)


def device_parts(plan, d):
    gx = quot(d, plan.along)
    gy = d - gx * plan.along
    level = quot(gy, plan.low)
    place = gx * plan.low + (gy - level * plan.low)
    return level, place


def send_positions(plan, entries):
    home_cap = plan.home_cap
    live = entries >= 0
    owner = jnp.where(live, entries >> OWN_SHIFT, plan.devices)
    named = lax.broadcasted_iota(jnp.int32, (plan.devices, home_cap), 0) == owner
    earlier = jnp.dot(
        jnp.where(named, 1.0, 0.0).astype(jnp.bfloat16),
        before_matrix(home_cap),
        preferred_element_type=jnp.float32,
    )
    rank = jnp.sum(jnp.where(named, earlier, 0.0), axis=0, keepdims=True).astype(jnp.int32)
    position = owner * plan.direct + rank
    if plan.extra:
        level, place = device_parts(plan, owner)
        later = (
            plan.devices * plan.direct
            + (place * plan.levels + level) * plan.extra
            + rank
            - plan.direct
        )
        position = jnp.where(rank < plan.direct, position, later)
    return jnp.where(live, position, plan.slots)


def column_sum(x):
    return jnp.sum(x, axis=1, keepdims=True)


def same_level_before(plan):
    shape = (plan.devices, plan.devices)
    level_r, place_r = device_parts(plan, lax.broadcasted_iota(jnp.int32, shape, 0))
    level_c, place_c = device_parts(plan, lax.broadcasted_iota(jnp.int32, shape, 1))
    return jnp.where((level_r == level_c) & (place_c < place_r), 1.0, 0.0).astype(jnp.bfloat16)


def extra_start(plan, before, over):
    wide = jnp.broadcast_to(over, (plan.devices, LANES)).astype(jnp.bfloat16)
    start = jnp.dot(before, wide, preferred_element_type=jnp.float32)
    return start[:, 0:1]


def arrival_matrix(plan, lists, me, my_level):
    devices, home_cap, direct = plan.devices, plan.home_cap, plan.direct
    mine = (lists >= 0) & ((lists >> OWN_SHIFT) == me)
    flags = jnp.where(mine, 1.0, 0.0)
    earlier = jnp.dot(
        flags.astype(jnp.bfloat16), before_matrix(home_cap), preferred_element_type=jnp.float32
    )
    rank = jnp.where(mine, earlier.astype(jnp.int32), plan.cap)
    slot = ((lists & (OWN_BLK - 1)) + 1).astype(jnp.float32)
    home = lax.broadcasted_iota(jnp.int32, (devices, 1), 0)
    if plan.extra:
        over = jnp.maximum(column_sum(flags) - direct, 0.0)
        start = extra_start(plan, same_level_before(plan), over).astype(jnp.int32)
        level, place = device_parts(plan, home)
    lane = lax.broadcasted_iota(jnp.int32, (devices, plan.padded), 1)
    spread = jnp.zeros((devices, plan.padded), jnp.float32)
    for i in range(plan.cap):
        code = column_sum(jnp.where(rank == i, slot, 0.0))
        if i < direct:
            at = home * direct + i
        else:
            near = devices * direct + place * plan.extra + i - direct
            within = start + i - direct
            far = devices * direct + plan.places * plan.extra + level * plan.room + within
            far = jnp.where(within < plan.room, far, plan.padded)
            at = jnp.where(level == my_level, near, far)
        spread = jnp.where((lane == at) & (code > 0.0), code, spread)
    row = jnp.sum(spread, axis=0, keepdims=True).astype(jnp.int32) - 1
    return onehot_rows(row, OWN_BLK)


def relay_matrix(plan, lists, my_level, my_place):
    devices, levels, extra, room = plan.devices, plan.levels, plan.extra, plan.room
    before = same_level_before(plan)
    columns = plan.places * levels * extra
    lane = lax.broadcasted_iota(jnp.int32, (devices, columns), 1)
    lane_place = quot(lane, levels * extra)
    lane_level = quot(lane - lane_place * (levels * extra), extra)
    lane_item = lane - (lane_place * levels + lane_level) * extra
    home = lax.broadcasted_iota(jnp.int32, (devices, 1), 0)
    home_level, home_place = device_parts(plan, home)
    place_gx = my_place // plan.low
    place_gy = my_place % plan.low
    spread = jnp.zeros((devices, columns), jnp.float32)
    for level in range(levels):
        owner = place_gx * plan.along + level * plan.low + place_gy
        named = (lists >= 0) & ((lists >> OWN_SHIFT) == owner)
        over = jnp.maximum(column_sum(jnp.where(named, 1.0, 0.0)) - plan.direct, 0.0)
        start = extra_start(plan, before, over)
        within = start + lane_item.astype(jnp.float32)
        ok = (
            (home_level == my_level)
            & (home_place == lane_place)
            & (lane_level == level)
            & (lane_item.astype(jnp.float32) < over)
            & (within < room)
        )
        spread = jnp.where(ok, within + (level * room + 1), spread)
    row = jnp.sum(spread, axis=0, keepdims=True).astype(jnp.int32) - 1
    return onehot_rows(row, levels * room)


def faces(c_low, c_high, k_low, k_high):
    courant = 0.5 * (c_low + c_high)
    diffuse = 0.5 * (k_low + k_high)
    return jnp.maximum(courant, 0.0) + diffuse, jnp.minimum(courant, 0.0) - diffuse


def stencil(plan, ext, mid, coef, cond_ref, out_ref):
    width, merged = plan.width, plan.merged
    lanes = merged + 2 * LANES
    core = slice(LANES, LANES + merged)
    chunks = range(ROW0 - 8, ROW0 + width + 8, 8)
    z = (lax.broadcasted_iota(jnp.int32, (8, lanes), 1) + (NZ - LANES % NZ)) % NZ
    top = z == NZ - 1
    bottom = z == 0

    def ahead(v, n):
        return pltpu.roll(v, lanes - n, 1)

    def behind(v, n):
        return pltpu.roll(v, n, 1)

    def coefficients():
        for base in chunks:
            rows = slice(base, base + 8)
            up = slice(base + 1, base + 9)
            down = slice(base - 1, base + 7)
            k0 = ext[8, rows, :]
            u0 = ext[5, rows, :]
            p, n = faces(u0, ext[5, up, :], k0, ext[8, up, :])
            p_low, n_low = faces(ext[5, down, :], u0, ext[8, down, :], k0)
            centre = 1.0 - (p - n_low)
            coef[0, rows, :] = -n
            coef[1, rows, :] = p_low
            v0 = ext[6, rows, :]
            p, n = faces(v0, ahead(v0, NZ), k0, ahead(k0, NZ))
            centre = centre - (p - behind(n, NZ))
            coef[2, rows, :] = -n
            coef[3, rows, :] = behind(p, NZ)
            w0 = ext[7, rows, :]
            p, n = faces(w0, ahead(w0, 1), k0, ahead(k0, 1))
            p = jnp.where(top, 0.0, p)
            n = jnp.where(top, 0.0, n)
            coef[4, rows, :] = -n
            p_low = jnp.where(bottom, 0.0, behind(p, 1))
            n_low = jnp.where(bottom, 0.0, behind(n, 1))
            coef[5, rows, :] = p_low
            coef[6, rows, :] = centre - (p - n_low)

    def update(src, f, base):
        rows = slice(base, base + 8)
        mine = src[f, rows, :]
        new = coef[6, rows, :] * mine
        new += coef[0, rows, :] * src[f, base + 1 : base + 9, :]
        new += coef[1, rows, :] * src[f, base - 1 : base + 7, :]
        new += coef[2, rows, :] * ahead(mine, NZ)
        new += coef[3, rows, :] * behind(mine, NZ)
        new += coef[4, rows, :] * ahead(mine, 1)
        new += coef[5, rows, :] * behind(mine, 1)
        return new

    def first(f, carry):
        for base in chunks:
            mid[f, base : base + 8, :] = update(ext, f, base)
        return carry

    def advance_once():
        lax.fori_loop(0, 5, first, 0)

    def second(f, carry):
        share = jnp.where(f == 0, 0.25, jnp.where(f == 1, -0.1, 0.0))
        for base in range(ROW0, ROW0 + width, 8):
            at = slice(base - ROW0, base - ROW0 + 8)
            out_ref[f, at, :] = update(mid, f, base)[:, core] + share * cond_ref[at, :]
        return carry

    def advance_twice():
        lax.fori_loop(0, 5, second, 0)

    return coefficients, advance_once, advance_twice


def grow_drops(plan, entries_ref, cells_ref, ext, drops, tab, hot, radius_out, mass):
    width = plan.width
    groups = plan.merged // GROUP
    used = groups * width
    for f in range(2):
        for g in range(groups):
            lanes = slice(LANES + g * GROUP, LANES + (g + 1) * GROUP)
            high, low = split(ext[f, ROW0 : ROW0 + width, lanes])
            tab[g * width : (g + 1) * width, 2 * f * GROUP : (2 * f + 1) * GROUP] = high
            tab[g * width : (g + 1) * width, (2 * f + 1) * GROUP : (2 * f + 2) * GROUP] = low
    if tab.shape[0] > used:
        tab[used:, :] = jnp.zeros((tab.shape[0] - used, tab.shape[1]), jnp.bfloat16)
    live_count = jnp.sum(
        jnp.where(entries_ref[...] >= 0, 1.0, 0.0), axis=1, keepdims=True
    ).astype(jnp.int32)

    def in_group(rows):
        c = cells_ref[rows, :]
        return c, quot(c[:, 0:1], GROUP)

    def one(g, carry):
        at = pl.multiple_of(g * BATCH, BATCH)
        rows = pl.ds(at, BATCH)
        c, q = in_group(rows)
        x = quot(q, groups)
        key = (q - x * groups) * width + x
        lane = lax.broadcasted_iota(jnp.int32, (BATCH, hot.shape[1]), 1)
        chosen = jnp.where(lane == key, 1.0, 0.0).astype(jnp.bfloat16)
        hot[rows, :] = chosen
        both = jnp.dot(chosen, tab[...], preferred_element_type=jnp.float32)
        offset = c - q * GROUP
        part = offset >> 7
        within = offset & (LANES - 1)

        def look(f):
            high = both[:, 2 * f * GROUP : (2 * f + 1) * GROUP]
            value = high + both[:, (2 * f + 1) * GROUP : (2 * f + 2) * GROUP]
            got = jnp.take_along_axis(value[:, :LANES], within, axis=1)
            for t in range(1, SPAN):
                tile = value[:, t * LANES : (t + 1) * LANES]
                got = jnp.where(part == t, jnp.take_along_axis(tile, within, axis=1), got)
            return got

        theta, vapour = look(0), look(1)
        supersat = vapour - 0.5 * jnp.tanh(theta)
        growth_rate = 1.0 / (1.0 + 0.1 * theta * theta)
        start = drops[0, rows, :]
        solute = drops[1, rows, :]
        weight = drops[2, rows, :]
        square = start * start
        for _ in range(SUBSTEPS):
            radius = jnp.sqrt(square)
            square = jnp.maximum(
                square
                + 0.05
                * growth_rate
                * (supersat - 0.02 / radius + solute / (radius * radius * radius)),
                0.04,
            )
        radius = jnp.sqrt(square)
        radius_out[rows, :] = radius
        grown = weight * (radius * square - start * start * start)
        block = at + lax.broadcasted_iota(jnp.int32, (BATCH, LANES), 0)
        mass[rows, :] = jnp.where(block < live_count, grown, 0.0)
        return carry

    lax.fori_loop(0, plan.home_cap // BATCH, one, 0)


def condense(plan, cells_ref, hot, mass, spread, cond):
    width = plan.width
    groups = plan.merged // GROUP
    row = lax.broadcasted_iota(jnp.int32, (LANES, LANES), 0)
    column = lax.broadcasted_iota(jnp.int32, (LANES, LANES), 1)
    upper = (row <= column).astype(jnp.float32)
    mass[...] = jnp.dot(
        mass[...], upper, precision=lax.Precision.HIGHEST, preferred_element_type=jnp.float32
    )
    lane = lax.broadcasted_iota(jnp.int32, (BATCH, LANES), 1)

    def sums(g, carry):
        rows = pl.ds(pl.multiple_of(g * BATCH, BATCH), BATCH)
        c = cells_ref[rows, :]
        offset = c - quot(c[:, 0:1], GROUP) * GROUP
        column = quot(offset[:, 0:1], NZ)
        level = offset - column * NZ
        count = jnp.zeros((BATCH, LANES), jnp.int32)
        step = LANES
        while step >= 1:
            probe = jnp.minimum(count + (step - 1), LANES - 1)
            below = jnp.take_along_axis(level, probe, axis=1) <= lane
            count = jnp.where(below & (count + step <= LANES), count + step, count)
            step //= 2
        upto = jnp.take_along_axis(mass[rows, :], jnp.maximum(count - 1, 0), axis=1)
        upto = jnp.where(count > 0, upto, 0.0)
        before = jnp.where(lane == 0, 0.0, pltpu.roll(upto, 1, 1))
        picked = upto - before
        for t in range(SPAN):
            place = lane + t * LANES
            which = quot(place, NZ)
            here = jnp.take_along_axis(picked, place - which * NZ, axis=1)
            high, low = split(jnp.where(which == column, here, 0.0))
            spread[rows, t * LANES : (t + 1) * LANES] = high
            spread[rows, GROUP + t * LANES : GROUP + (t + 1) * LANES] = low
        return carry

    lax.fori_loop(0, plan.home_cap // BATCH, sums, 0)
    both = lax.dot_general(
        hot[...], spread[...], (((0,), (0,)), ((), ())), preferred_element_type=jnp.float32
    )
    for g in range(groups):
        rows = slice(g * width, (g + 1) * width)
        cond[:, g * GROUP : (g + 1) * GROUP] = both[rows, :GROUP] + both[rows, GROUP:]


def main_kernel(
    plan,
    entries_ref,
    cells_ref,
    fields_hbm,
    winds_hbm,
    diff_hbm,
    planes_hbm,
    fields_hbm_out,
    drops_hbm_out,
    radius_out,
    flag_out,
    fields_out,
    drops_out,
    out_sem,
    ext,
    mid,
    coef,
    cond,
    drops,
    lists,
    pack_hot,
    relay_hot,
    place_hot,
    tab,
    hot,
    mass,
    spread,
    x_send,
    x_recv,
    y_send,
    y_recv,
    load_sem,
    grid_sem,
    list_sem,
    halo_send,
    halo_recv,
    *chunk_refs,
):
    devices, across, along = plan.devices, plan.across, plan.along
    low, levels, places = plan.low, plan.levels, plan.places
    direct, extra, room = plan.direct, plan.extra, plan.room
    width, merged = plan.width, plan.merged
    count = len(CHUNKS)
    per = 6 if extra else 2
    buffers = [chunk_refs[i * per : (i + 1) * per] for i in range(count)]
    sems = chunk_refs[count * per :]
    gx = lax.axis_index("gx")
    gy = lax.axis_index("gy")
    me = gx * along + gy
    my_level = gy // low
    my_place = gx * low + gy % low
    barrier = pltpu.get_barrier_semaphore()

    def device(d):
        return {"gx": d // along, "gy": d % along}

    def greet(s, carry):
        other = (me + s) % devices
        pl.semaphore_signal(barrier, inc=1, device_id=device(other), device_id_type=MESH)
        return carry

    lax.fori_loop(1, devices, greet, 0)

    loads = []
    for i, (at, n) in enumerate(LOADS):
        rows = pl.ds(at, n)
        loads.append(pltpu.make_async_copy(planes_hbm.at[rows], drops.at[rows], load_sem.at[i]))
    own_rows = pl.ds(ROW0, width)
    own_lanes = pl.ds(LANES, merged)
    grids = (
        pltpu.make_async_copy(
            fields_hbm, ext.at[pl.ds(0, 5), own_rows, own_lanes], grid_sem.at[0]
        ),
        pltpu.make_async_copy(winds_hbm, ext.at[pl.ds(5, 3), own_rows, own_lanes], grid_sem.at[1]),
        pltpu.make_async_copy(diff_hbm, ext.at[8, own_rows, own_lanes], grid_sem.at[2]),
    )
    loads[0].start()
    for grid in grids:
        grid.start()
    loads[1].start()
    loads[2].start()

    pack_hot[...] = onehot_rows(send_positions(plan, entries_ref[...]), plan.slots)
    pl.semaphore_wait(barrier, devices - 1)

    def remote(src, dst, send_sem, recv_sem, to):
        return pltpu.make_async_remote_copy(
            src_ref=src,
            dst_ref=dst,
            send_sem=send_sem,
            recv_sem=recv_sem,
            device_id=to,
            device_id_type=MESH,
        )

    halos = []

    def halo(src, dst, dx, dy):
        i = len(halos)
        to = {"gx": (gx + dx + across) % across, "gy": (gy + dy + along) % along}
        copy = remote(src, dst, halo_send.at[i], halo_recv.at[i], to)
        copy.start()
        halos.append(copy)

    left_lanes = pl.ds(0, LANES)
    right_lanes = pl.ds(LANES + merged, LANES)
    begin, end = pl.ds(0, LANES), pl.ds(merged - LANES, LANES)

    def y_halos():
        for grid in grids:
            grid.wait()
        rows = slice(ROW0, ROW0 + width)
        for side, dy in ((0, -1), (1, 1)):
            pieces = []
            for k, n in Y_EDGE:
                at = LANES if side == 0 else LANES + merged - n * NZ
                pieces.append(ext[k, rows, at : at + n * NZ])
            y_send[side] = jnp.concatenate(pieces, axis=1)
            halo(y_send.at[side], y_recv.at[1 - side], 0, dy)

    def y_arrived():
        rows = slice(ROW0, ROW0 + width)
        for side in range(2):
            edge = y_recv[side]
            at = 0
            for k, n in Y_EDGE:
                to = LANES - n * NZ if side == 0 else LANES + merged
                ext[k, rows, to : to + n * NZ] = edge[:, at : at + n * NZ]
                at += n * NZ

    def x_halos():
        for k in range(9):
            x_send[0, k] = ext[k, ROW0 : ROW0 + 2, LANES : LANES + merged]
            x_send[1, k] = ext[k, ROW0 + width - 2 : ROW0 + width, LANES : LANES + merged]
        every, both = pl.ds(0, 9), pl.ds(0, 2)
        for side, dx in ((0, -1), (1, 1)):
            to = x_recv.at[1 - side]
            halo(x_send.at[side], to.at[every, both, own_lanes], dx, 0)
            halo(x_send.at[side, every, both, begin], to.at[every, both, right_lanes], dx, -1)
            halo(x_send.at[side, every, both, end], to.at[every, both, left_lanes], dx, 1)

    my_lists = pl.ds(my_place * levels, levels)

    def tell_levels(s, carry):
        level = (my_level + s) % levels
        to = {"gx": gx, "gy": level * low + gy % low}
        at = lists.at[my_place * levels + my_level]
        remote(entries_ref, at, list_sem.at[0], list_sem.at[1], to).start()
        return carry

    def tell_places(s, carry):
        place = (my_place + s) % places
        to = {"gx": place // low, "gy": my_level * low + place % low}
        mine = lists.at[my_lists]
        remote(mine, mine, list_sem.at[2], list_sem.at[3], to).start()
        return carry

    def pack(c):
        near, far = buffers[c][0], buffers[c][2] if extra else None
        for r, attribute in enumerate(CHUNKS[c]):
            if attribute == 0:
                value = radius_out[...]
            else:
                value = drops[attribute]
                if 3 <= attribute < 6:
                    value = value + 0.1 * drops[attribute + 3]
            packed = pick(pack_hot[...], value)
            cut = devices * direct
            near[:, r * direct : (r + 1) * direct, :] = packed[:cut].reshape(
                devices, direct, LANES
            )
            if extra:
                n = levels * extra
                far[:, r * n : (r + 1) * n, :] = packed[cut:].reshape(places, n, LANES)

    def send(c):
        near, near_in = buffers[c][0:2]
        if extra:
            far, far_in = buffers[c][2:4]

            def give(s, carry):
                place = (my_place + s) % places
                to = {"gx": place // low, "gy": my_level * low + place % low}
                remote(
                    far.at[place], far_in.at[my_place], sems[2].at[c], sems[3].at[c], to
                ).start()
                return carry

            lax.fori_loop(1, places, give, 0)
            far_in[my_place] = far[my_place]

        def out(s, carry):
            other = (me + s) % devices
            remote(
                near.at[other], near_in.at[me], sems[0].at[c], sems[1].at[c], device(other)
            ).start()
            return carry

        lax.fori_loop(1, devices, out, 0)
        near_in[me] = near[me]

    def wait_all(ref, n, sem):
        part = ref.at[pl.ds(0, n)]
        pltpu.make_async_copy(part, part, sem).wait()

    def relay(c):
        far_in, onward, onward_in = buffers[c][3:6]
        wait_all(far_in, places - 1, sems[3].at[c])
        n = levels * extra
        for r in range(len(CHUNKS[c])):
            rows = far_in[:, r * n : (r + 1) * n, :].reshape(places * n, LANES)
            onward[:, r * room : (r + 1) * room, :] = pick(relay_hot[...], rows).reshape(
                levels, room, LANES
            )

        def pass_on(s, carry):
            level = (my_level + s) % levels
            to = {"gx": gx, "gy": level * low + gy % low}
            remote(
                onward.at[level], onward_in.at[my_level], sems[4].at[c], sems[5].at[c], to
            ).start()
            return carry

        lax.fori_loop(1, levels, pass_on, 0)
        onward_in[my_level] = jnp.zeros(onward_in.shape[1:], jnp.float32)

    loads[0].wait()
    lists[my_place * levels + my_level] = entries_ref[...]
    lax.fori_loop(1, levels, tell_levels, 0)
    pack(0)
    send(0)
    y_halos()
    x_halos()
    loads[1].wait()
    loads[2].wait()
    pack(1)
    send(1)
    wait_all(lists, levels - 1, list_sem.at[1])
    lax.fori_loop(1, places, tell_places, 0)
    grow_drops(plan, entries_ref, cells_ref, ext, drops, tab, hot, radius_out, mass)
    pack(2)
    send(2)
    condense(plan, cells_ref, hot, mass, spread, cond)

    for copy in halos:
        copy.wait()
    y_arrived()
    for k in range(9):
        ext[k, ROW0 - 2 : ROW0, :] = x_recv[0, k]
        ext[k, ROW0 + width : ROW0 + width + 2, :] = x_recv[1, k]
    coefficients, advance_once, advance_twice = stencil(plan, ext, mid, coef, cond, fields_out)
    coefficients()

    wait_all(lists, (places - 1) * levels, list_sem.at[3])

    def list_of(d):
        place = (d // along) * low + d % low
        return lists[place * levels + (d % along) // low]

    known = jnp.concatenate([list_of(d) for d in range(devices)], axis=0)
    if extra:
        relay_hot[...] = relay_matrix(plan, known, my_level, my_place)
        relay(0)
        relay(1)
    advance_once()
    if extra:
        relay(2)
    place_hot[...] = arrival_matrix(plan, known, me, my_level)
    advance_twice()
    finished = []

    def finish(which, src, dst, i):
        copy = pltpu.make_async_copy(src.at[i], dst.at[i], out_sem.at[which, i])
        copy.start()
        finished.append(copy)

    for f in range(5):
        finish(0, fields_out, fields_hbm_out, f)

    if extra:
        flag = jnp.zeros((devices, 1), jnp.float32)
        totals = [flag] * levels
        owner = lax.broadcasted_iota(jnp.int32, (devices, plan.home_cap), 0)
        for d in range(devices):
            counts = column_sum(jnp.where((list_of(d) >> OWN_SHIFT) == owner, 1.0, 0.0))
            level = (d % along) // low
            totals[level] = totals[level] + jnp.maximum(counts - direct, 0.0)
        for total in totals:
            flag = jnp.maximum(flag, jnp.where(total > room, 1.0, 0.0))
        flag_out[0] = jnp.max(flag).astype(jnp.int32)
    else:
        flag_out[0] = 0

    for c in range(count):
        near_in = buffers[c][1]
        wait_all(near_in, devices - 1, sems[1].at[c])
        if extra:
            far_in, onward_in = buffers[c][3], buffers[c][5]
            wait_all(onward_in, levels - 1, sems[5].at[c])
        for r, attribute in enumerate(CHUNKS[c]):
            parts = [
                near_in[:, r * direct : (r + 1) * direct, :].reshape(devices * direct, LANES)
            ]
            if extra:
                at = pl.multiple_of((r * levels + my_level) * extra, 8)
                parts.append(far_in[:, pl.ds(at, extra), :].reshape(places * extra, LANES))
                parts.append(
                    onward_in[:, r * room : (r + 1) * room, :].reshape(levels * room, LANES)
                )
            if plan.padded > plan.arrivals:
                parts.append(jnp.zeros((plan.padded - plan.arrivals, LANES), jnp.float32))
            rows = jnp.concatenate(parts, axis=0) if len(parts) > 1 else parts[0]
            drops_out[attribute] = pick(place_hot[...], rows)
            finish(1, drops_out, drops_hbm_out, attribute)

    for copy in finished:
        copy.wait()
    wait_all(lists, levels - 1, list_sem.at[0])
    wait_all(lists, (places - 1) * levels, list_sem.at[2])
    for c in range(count):
        wait_all(buffers[c][0], devices - 1, sems[0].at[c])
        if extra:
            wait_all(buffers[c][2], places - 1, sems[2].at[c])
            wait_all(buffers[c][4], levels - 1, sems[4].at[c])


def run_main(plan, entries, cells, fields, winds, diffusion, planes):
    width, merged, home_cap = plan.width, plan.merged, plan.home_cap
    tall = ROW0 + width + 16
    wide = merged + 2 * LANES
    groups = merged // GROUP
    keys = -(-groups * width // LANES) * LANES
    f32, bf16 = jnp.float32, jnp.bfloat16
    buffers = []
    for chunk in CHUNKS:
        n = len(chunk)
        near = pltpu.VMEM((plan.devices, n * plan.direct, LANES), f32)
        buffers += [near, near]
        if plan.extra:
            far = pltpu.VMEM((plan.places, n * plan.levels * plan.extra, LANES), f32)
            onward = pltpu.VMEM((plan.levels, n * plan.room, LANES), f32)
            buffers += [far, far, onward, onward]
    sem = pltpu.SemaphoreType.DMA((len(CHUNKS),))
    relay_shape = (16, LANES)
    if plan.extra:
        relay_shape = (plan.levels * plan.room, plan.places * plan.levels * plan.extra)
    return pl.pallas_call(
        lambda *refs: main_kernel(plan, *refs),
        out_shape=(
            jax.ShapeDtypeStruct(fields.shape, f32),
            jax.ShapeDtypeStruct((planes.shape[0], OWN_BLK, LANES), f32),
            jax.ShapeDtypeStruct((home_cap, LANES), f32),
            jax.ShapeDtypeStruct((1,), jnp.int32),
        ),
        in_specs=[VMEM, VMEM, ANY, ANY, ANY, ANY],
        out_specs=(ANY, ANY, VMEM, SMEM),
        scratch_shapes=[
            pltpu.VMEM(fields.shape, f32),
            pltpu.VMEM((planes.shape[0], OWN_BLK, LANES), f32),
            pltpu.SemaphoreType.DMA((2, max(planes.shape[0], fields.shape[0]))),
            pltpu.VMEM((9, tall, wide), f32),
            pltpu.VMEM((5, tall, wide), f32),
            pltpu.VMEM((7, tall, wide), f32),
            pltpu.VMEM((width, merged), f32),
            pltpu.VMEM(planes.shape, f32),
            pltpu.VMEM((plan.devices, 1, home_cap), jnp.int32),
            pltpu.VMEM((plan.slots, home_cap), bf16),
            pltpu.VMEM(relay_shape, bf16),
            pltpu.VMEM((OWN_BLK, plan.padded), bf16),
            pltpu.VMEM((keys, 4 * GROUP), bf16),
            pltpu.VMEM((home_cap, keys), bf16),
            pltpu.VMEM((home_cap, LANES), f32),
            pltpu.VMEM((home_cap, 2 * GROUP), bf16),
            pltpu.VMEM((2, 9, 2, merged), f32),
            pltpu.VMEM((2, 9, 2, wide), f32),
            pltpu.VMEM((2, width, sum(n for _, n in Y_EDGE) * NZ), f32),
            pltpu.VMEM((2, width, sum(n for _, n in Y_EDGE) * NZ), f32),
            pltpu.SemaphoreType.DMA((len(LOADS),)),
            pltpu.SemaphoreType.DMA((3,)),
            pltpu.SemaphoreType.DMA((4,)),
            pltpu.SemaphoreType.DMA((8,)),
            pltpu.SemaphoreType.DMA((8,)),
            *buffers,
            *([sem] * (6 if plan.extra else 2)),
        ],
        compiler_params=pltpu.CompilerParams(
            vmem_limit_bytes=LIMIT, collective_id=0, has_side_effects=True
        ),
        cost_estimate=cost(16 << 20, 1 << 28),
        name="condense_advance",
    )(entries, cells, fields, winds, diffusion, planes)


def hand_kernel(fields_ref, drops_ref, fields_out, drops_out, fields_held, drops_held, sem):
    arrays = ((fields_ref, fields_held, fields_out), (drops_ref, drops_held, drops_out))
    pieces = [(a, i) for a in arrays for i in range(a[0].shape[0])]

    def move(n, step):
        refs, i = pieces[n]
        return pltpu.make_async_copy(refs[step].at[i], refs[step + 1].at[i], sem.at[step, n])

    for n in range(len(pieces)):
        move(n, 0).start()
    for n in range(len(pieces)):
        move(n, 0).wait()
        move(n, 1).start()
    for n in range(len(pieces)):
        move(n, 1).wait()


def hand_over(fields, drops):
    return pl.pallas_call(
        hand_kernel,
        out_shape=(
            jax.ShapeDtypeStruct(fields.shape, jnp.float32),
            jax.ShapeDtypeStruct(drops.shape, jnp.float32),
        ),
        in_specs=[ANY, ANY],
        out_specs=(ANY, ANY),
        scratch_shapes=[
            pltpu.VMEM(fields.shape, jnp.float32),
            pltpu.VMEM(drops.shape, jnp.float32),
            pltpu.SemaphoreType.DMA((2, fields.shape[0] + drops.shape[0])),
        ],
        compiler_params=pltpu.CompilerParams(vmem_limit_bytes=LIMIT),
        cost_estimate=cost(8 << 20, 1 << 10),
        name="hand_over",
    )(fields, drops)


def resend(plan, balance_list, planes, radius):
    everyone = ("gx", "gy")
    devices, cap = plan.devices, plan.cap
    count = planes.shape[0]

    def exchange(x):
        return lax.all_to_all(x, everyone, split_axis=0, concat_axis=0, tiled=True)

    outgoing = pack_drops(
        balance_list.reshape(1, plan.home_cap),
        jnp.concatenate([planes, radius[None]], axis=0),
        devices,
        cap,
    )
    lists = lax.all_gather(balance_list, everyone)
    codes = arrival_codes(lax.axis_index(everyone).reshape(1), lists, cap)
    return place_drops(codes, exchange(outgoing), count)


def per_device(fields, winds, diffusion, droplets, cells, balance_list):
    width = fields.shape[1]
    merged = fields.shape[2]
    home_cap = balance_list.shape[0]
    plan = Plan((lax.axis_size("gx"), lax.axis_size("gy")), home_cap, width, merged)
    planes = droplets.transpose(1, 0, 2)
    fields_out, placed, radius, flag = run_main(
        plan, balance_list.reshape(1, home_cap), cells, fields, winds, diffusion, planes
    )
    fields_out, placed = hand_over(fields_out, placed)
    if plan.extra:
        placed = lax.cond(
            flag[0] > 0,
            lambda: resend(plan, balance_list, planes, radius),
            lambda: placed,
        )
    return (fields_out, placed.transpose(1, 0, 2))


def solution(mesh):
    return jax.shard_map(
        per_device,
        mesh=mesh,
        in_specs=(
            P(None, "gx", "gy"),
            P(None, "gx", "gy"),
            P("gx", "gy"),
            P(("gx", "gy"), None, None),
            P(("gx", "gy"), None),
            P(("gx", "gy")),
        ),
        out_specs=(P(None, "gx", "gy"), P(("gx", "gy"), None, None)),
        check_vma=False,
    )
```

```python
import math

import jax
import jax.numpy as jnp
from jax import lax
from jax.experimental import pallas as pl
from jax.experimental.pallas import tpu as pltpu
from jax.sharding import PartitionSpec as P

NZ = 48
OWN_BLK = 256
SUBSTEPS = 4
LANES = 128
ROW0 = 16
BATCH = 64
OWN_SHIFT = OWN_BLK.bit_length() - 1
GROUP = math.lcm(NZ, LANES)
SPAN = GROUP // LANES
DIRECT = 8
ROOM = 40
CHUNKS = ((9, 10, 11), (1, 2, 6, 7), (8, 3, 4, 5, 0))
LOADS = ((9, 3), (0, 3), (3, 6))
Y_EDGE = ((0, 2), (1, 2), (2, 2), (3, 2), (4, 2), (6, 2), (8, 2), (5, 1), (7, 1))
VMEM = pl.BlockSpec(memory_space=pltpu.VMEM)
SMEM = pl.BlockSpec(memory_space=pltpu.SMEM)
ANY = pl.BlockSpec(memory_space=pl.ANY)
MESH = pl.DeviceIdType.MESH
LIMIT = 56 * 1024 * 1024


def cost(bytes_accessed, flops):
    return pl.CostEstimate(flops=flops, bytes_accessed=bytes_accessed, transcendentals=0)


def split(x):
    high = x.astype(jnp.bfloat16)
    return high, (x - high.astype(jnp.float32)).astype(jnp.bfloat16)


def pick(onehot, x):
    both = jnp.concatenate(split(x), axis=1)
    out = jnp.dot(onehot, both, preferred_element_type=jnp.float32)
    return out[:, :LANES] + out[:, LANES:]


def before_matrix(count):
    row = lax.broadcasted_iota(jnp.int32, (count, count), 0)
    column = lax.broadcasted_iota(jnp.int32, (count, count), 1)
    return jnp.where(row < column, 1.0, 0.0).astype(jnp.bfloat16)


def positions(entries, devices, send_cap):
    home_cap = entries.shape[1]
    owner = jnp.where(entries >= 0, entries >> OWN_SHIFT, devices)
    named = lax.broadcasted_iota(jnp.int32, (devices, home_cap), 0) == owner
    earlier = jnp.dot(
        jnp.where(named, 1.0, 0.0).astype(jnp.bfloat16),
        before_matrix(home_cap),
        preferred_element_type=jnp.float32,
    )
    rank = jnp.sum(jnp.where(named, earlier, 0.0), axis=0, keepdims=True).astype(jnp.int32)
    return jnp.where(entries >= 0, owner * send_cap + rank, devices * send_cap)


def onehot_rows(index, count):
    row = lax.broadcasted_iota(jnp.int32, (count, index.shape[1]), 0)
    return jnp.where(row == index, 1.0, 0.0).astype(jnp.bfloat16)


def pack_kernel(devices, send_cap, entries_ref, drops_ref, moves_ref, out_ref, onehot):
    step = pl.program_id(0)

    @pl.when(step == 0)
    def _():
        position = positions(entries_ref[...], devices, send_cap)
        onehot[...] = onehot_rows(position, devices * send_cap)

    rate = jnp.where((step >= 2) & (step < 5), 0.1, 0.0)
    packed = pick(onehot[...], drops_ref[0] + rate * moves_ref[0])
    out_ref[...] = packed.reshape(devices, send_cap, LANES)


def pack_drops(entries, planes, devices, send_cap):
    count, home_cap, _ = planes.shape
    total = devices * send_cap
    last = count - 1
    return pl.pallas_call(
        lambda *refs: pack_kernel(devices, send_cap, *refs),
        grid=(count - 1,),
        out_shape=jax.ShapeDtypeStruct((devices, (count - 1) * send_cap, LANES), jnp.float32),
        in_specs=[
            pl.BlockSpec((1, home_cap), lambda i: (0, 0)),
            pl.BlockSpec((1, home_cap, LANES), lambda i: (i + 1, 0, 0)),
            pl.BlockSpec((1, home_cap, LANES), lambda i: (jnp.minimum(i + 4, last), 0, 0)),
        ],
        out_specs=pl.BlockSpec((devices, send_cap, LANES), lambda i: (0, i, 0)),
        scratch_shapes=[pltpu.VMEM((total, home_cap), jnp.bfloat16)],
        compiler_params=pltpu.CompilerParams(vmem_limit_bytes=24 * 1024 * 1024),
        cost_estimate=cost(6 << 20, 1 << 20),
        name="pack_drops",
    )(entries, planes, planes)


def codes_kernel(send_cap, me_ref, lists_ref, out_ref):
    homes, home_cap = lists_ref.shape
    entries = lists_ref[...]
    mine = (entries >= 0) & ((entries >> OWN_SHIFT) == me_ref[0])
    earlier = jnp.dot(
        jnp.where(mine, 1.0, 0.0).astype(jnp.bfloat16),
        before_matrix(home_cap),
        preferred_element_type=jnp.float32,
    )
    rank = jnp.where(mine, earlier.astype(jnp.int32), send_cap)
    slot = ((entries & (OWN_BLK - 1)) + 1).astype(jnp.float32)
    lane = lax.broadcasted_iota(jnp.int32, (homes, homes * send_cap), 1)
    home = lax.broadcasted_iota(jnp.int32, (homes, homes * send_cap), 0)
    spread = jnp.zeros((homes, homes * send_cap), jnp.float32)
    for i in range(send_cap):
        code = jnp.sum(jnp.where(rank == i, slot, 0.0), axis=1, keepdims=True)
        spread = jnp.where(lane == home * send_cap + i, code, spread)
    out_ref[...] = jnp.sum(spread, axis=0, keepdims=True).astype(jnp.int32) - 1


def arrival_codes(me, lists, send_cap):
    homes = lists.shape[0]
    return pl.pallas_call(
        lambda *refs: codes_kernel(send_cap, *refs),
        out_shape=jax.ShapeDtypeStruct((1, homes * send_cap), jnp.int32),
        in_specs=[SMEM, VMEM],
        out_specs=VMEM,
        cost_estimate=cost(1 << 18, 1 << 22),
        name="arrival_codes",
    )(me, lists)


def place_kernel(codes_ref, arrived_ref, out_ref, onehot):
    total = codes_ref.shape[1]

    @pl.when(pl.program_id(0) == 0)
    def _():
        onehot[...] = onehot_rows(codes_ref[...], OWN_BLK)

    out_ref[0] = pick(onehot[...], arrived_ref[...].reshape(total, LANES))


def place_drops(codes, arrived, count):
    total = codes.shape[1]
    devices = arrived.shape[0]
    send_cap = total // devices
    return pl.pallas_call(
        place_kernel,
        grid=(count,),
        out_shape=jax.ShapeDtypeStruct((count, OWN_BLK, LANES), jnp.float32),
        in_specs=[
            pl.BlockSpec((1, total), lambda i: (0, 0)),
            pl.BlockSpec((devices, send_cap, LANES), lambda i: (0, (i + count - 1) % count, 0)),
        ],
        out_specs=pl.BlockSpec((1, OWN_BLK, LANES), lambda i: (i, 0, 0)),
        scratch_shapes=[pltpu.VMEM((OWN_BLK, total), jnp.bfloat16)],
        compiler_params=pltpu.CompilerParams(vmem_limit_bytes=16 * 1024 * 1024),
        cost_estimate=cost(5 << 20, 1 << 20),
        name="place_drops",
    )(codes, arrived)

class Plan:
    def __init__(self, axes, home_cap, width, merged):
        self.across, self.along = axes
        self.devices = self.across * self.along
        self.home_cap = home_cap
        self.width, self.merged = width, merged
        self.cap = -(-(home_cap // self.devices) // 8) * 8
        self.direct = min(DIRECT, self.cap)
        self.extra = self.cap - self.direct
        self.low = 2 if self.along % 2 == 0 else 1
        self.levels = self.along // self.low
        self.places = self.across * self.low
        self.room = min(ROOM, self.places * self.extra)
        self.slots = self.devices * self.cap
        arrivals = self.devices * self.direct
        if self.extra:
            arrivals += self.places * self.extra + self.levels * self.room
        self.arrivals = arrivals
        self.padded = -(-arrivals // LANES) * LANES


def quot(v, by):
    return ((v.astype(jnp.float32) + 0.5) * (1.0 / by)).astype(jnp.int32)


def device_parts(plan, d):
    gx = quot(d, plan.along)
    gy = d - gx * plan.along
    level = quot(gy, plan.low)
    place = gx * plan.low + (gy - level * plan.low)
    return level, place


def send_positions(plan, entries):
    home_cap = plan.home_cap
    live = entries >= 0
    owner = jnp.where(live, entries >> OWN_SHIFT, plan.devices)
    named = lax.broadcasted_iota(jnp.int32, (plan.devices, home_cap), 0) == owner
    earlier = jnp.dot(
        jnp.where(named, 1.0, 0.0).astype(jnp.bfloat16),
        before_matrix(home_cap),
        preferred_element_type=jnp.float32,
    )
    rank = jnp.sum(jnp.where(named, earlier, 0.0), axis=0, keepdims=True).astype(jnp.int32)
    position = owner * plan.direct + rank
    if plan.extra:
        level, place = device_parts(plan, owner)
        later = (
            plan.devices * plan.direct
            + (place * plan.levels + level) * plan.extra
            + rank
            - plan.direct
        )
        position = jnp.where(rank < plan.direct, position, later)
    return jnp.where(live, position, plan.slots)


def column_sum(x):
    return jnp.sum(x, axis=1, keepdims=True)


def same_level_before(plan):
    shape = (plan.devices, plan.devices)
    level_r, place_r = device_parts(plan, lax.broadcasted_iota(jnp.int32, shape, 0))
    level_c, place_c = device_parts(plan, lax.broadcasted_iota(jnp.int32, shape, 1))
    return jnp.where((level_r == level_c) & (place_c < place_r), 1.0, 0.0).astype(jnp.bfloat16)


def extra_start(plan, before, over):
    wide = jnp.broadcast_to(over, (plan.devices, LANES)).astype(jnp.bfloat16)
    start = jnp.dot(before, wide, preferred_element_type=jnp.float32)
    return start[:, 0:1]


def arrival_matrix(plan, lists, me, my_level):
    devices, home_cap, direct = plan.devices, plan.home_cap, plan.direct
    mine = (lists >= 0) & ((lists >> OWN_SHIFT) == me)
    flags = jnp.where(mine, 1.0, 0.0)
    earlier = jnp.dot(
        flags.astype(jnp.bfloat16), before_matrix(home_cap), preferred_element_type=jnp.float32
    )
    rank = jnp.where(mine, earlier.astype(jnp.int32), plan.cap)
    slot = ((lists & (OWN_BLK - 1)) + 1).astype(jnp.float32)
    home = lax.broadcasted_iota(jnp.int32, (devices, 1), 0)
    if plan.extra:
        over = jnp.maximum(column_sum(flags) - direct, 0.0)
        start = extra_start(plan, same_level_before(plan), over).astype(jnp.int32)
        level, place = device_parts(plan, home)
    lane = lax.broadcasted_iota(jnp.int32, (devices, plan.padded), 1)
    spread = jnp.zeros((devices, plan.padded), jnp.float32)
    for i in range(plan.cap):
        code = column_sum(jnp.where(rank == i, slot, 0.0))
        if i < direct:
            at = home * direct + i
        else:
            near = devices * direct + place * plan.extra + i - direct
            within = start + i - direct
            far = devices * direct + plan.places * plan.extra + level * plan.room + within
            far = jnp.where(within < plan.room, far, plan.padded)
            at = jnp.where(level == my_level, near, far)
        spread = jnp.where((lane == at) & (code > 0.0), code, spread)
    row = jnp.sum(spread, axis=0, keepdims=True).astype(jnp.int32) - 1
    return onehot_rows(row, OWN_BLK)


def relay_matrix(plan, lists, my_level, my_place):
    devices, levels, extra, room = plan.devices, plan.levels, plan.extra, plan.room
    before = same_level_before(plan)
    columns = plan.places * levels * extra
    lane = lax.broadcasted_iota(jnp.int32, (devices, columns), 1)
    lane_place = quot(lane, levels * extra)
    lane_level = quot(lane - lane_place * (levels * extra), extra)
    lane_item = lane - (lane_place * levels + lane_level) * extra
    home = lax.broadcasted_iota(jnp.int32, (devices, 1), 0)
    home_level, home_place = device_parts(plan, home)
    place_gx = my_place // plan.low
    place_gy = my_place % plan.low
    spread = jnp.zeros((devices, columns), jnp.float32)
    for level in range(levels):
        owner = place_gx * plan.along + level * plan.low + place_gy
        named = (lists >= 0) & ((lists >> OWN_SHIFT) == owner)
        over = jnp.maximum(column_sum(jnp.where(named, 1.0, 0.0)) - plan.direct, 0.0)
        start = extra_start(plan, before, over)
        within = start + lane_item.astype(jnp.float32)
        ok = (
            (home_level == my_level)
            & (home_place == lane_place)
            & (lane_level == level)
            & (lane_item.astype(jnp.float32) < over)
            & (within < room)
        )
        spread = jnp.where(ok, within + (level * room + 1), spread)
    row = jnp.sum(spread, axis=0, keepdims=True).astype(jnp.int32) - 1
    return onehot_rows(row, levels * room)


def faces(c_low, c_high, k_low, k_high):
    courant = 0.5 * (c_low + c_high)
    diffuse = 0.5 * (k_low + k_high)
    return jnp.maximum(courant, 0.0) + diffuse, jnp.minimum(courant, 0.0) - diffuse


def stencil(plan, ext, mid, coef, cond_ref, out_ref):
    width, merged = plan.width, plan.merged
    lanes = merged + 2 * LANES
    core = slice(LANES, LANES + merged)
    chunks = range(ROW0 - 8, ROW0 + width + 8, 8)
    z = (lax.broadcasted_iota(jnp.int32, (8, lanes), 1) + (NZ - LANES % NZ)) % NZ
    top = z == NZ - 1
    bottom = z == 0

    def ahead(v, n):
        return pltpu.roll(v, lanes - n, 1)

    def behind(v, n):
        return pltpu.roll(v, n, 1)

    def coefficients():
        for base in chunks:
            rows = slice(base, base + 8)
            up = slice(base + 1, base + 9)
            down = slice(base - 1, base + 7)
            k0 = ext[8, rows, :]
            u0 = ext[5, rows, :]
            p, n = faces(u0, ext[5, up, :], k0, ext[8, up, :])
            p_low, n_low = faces(ext[5, down, :], u0, ext[8, down, :], k0)
            centre = 1.0 - (p - n_low)
            coef[0, rows, :] = -n
            coef[1, rows, :] = p_low
            v0 = ext[6, rows, :]
            p, n = faces(v0, ahead(v0, NZ), k0, ahead(k0, NZ))
            centre = centre - (p - behind(n, NZ))
            coef[2, rows, :] = -n
            coef[3, rows, :] = behind(p, NZ)
            w0 = ext[7, rows, :]
            p, n = faces(w0, ahead(w0, 1), k0, ahead(k0, 1))
            p = jnp.where(top, 0.0, p)
            n = jnp.where(top, 0.0, n)
            coef[4, rows, :] = -n
            p_low = jnp.where(bottom, 0.0, behind(p, 1))
            n_low = jnp.where(bottom, 0.0, behind(n, 1))
            coef[5, rows, :] = p_low
            coef[6, rows, :] = centre - (p - n_low)

    def update(src, f, base):
        rows = slice(base, base + 8)
        mine = src[f, rows, :]
        new = coef[6, rows, :] * mine
        new += coef[0, rows, :] * src[f, base + 1 : base + 9, :]
        new += coef[1, rows, :] * src[f, base - 1 : base + 7, :]
        new += coef[2, rows, :] * ahead(mine, NZ)
        new += coef[3, rows, :] * behind(mine, NZ)
        new += coef[4, rows, :] * ahead(mine, 1)
        new += coef[5, rows, :] * behind(mine, 1)
        return new

    def first(f, carry):
        for base in chunks:
            mid[f, base : base + 8, :] = update(ext, f, base)
        return carry

    def advance_once():
        lax.fori_loop(0, 5, first, 0)

    def second(f, carry):
        share = jnp.where(f == 0, 0.25, jnp.where(f == 1, -0.1, 0.0))
        for base in range(ROW0, ROW0 + width, 8):
            at = slice(base - ROW0, base - ROW0 + 8)
            out_ref[f, at, :] = update(mid, f, base)[:, core] + share * cond_ref[at, :]
        return carry

    def advance_twice():
        lax.fori_loop(0, 5, second, 0)

    return coefficients, advance_once, advance_twice


def grow_drops(plan, entries_ref, cells_ref, ext, drops, tab, hot, radius_out, mass):
    width = plan.width
    groups = plan.merged // GROUP
    used = groups * width
    for f in range(2):
        for g in range(groups):
            lanes = slice(LANES + g * GROUP, LANES + (g + 1) * GROUP)
            high, low = split(ext[f, ROW0 : ROW0 + width, lanes])
            tab[g * width : (g + 1) * width, 2 * f * GROUP : (2 * f + 1) * GROUP] = high
            tab[g * width : (g + 1) * width, (2 * f + 1) * GROUP : (2 * f + 2) * GROUP] = low
    if tab.shape[0] > used:
        tab[used:, :] = jnp.zeros((tab.shape[0] - used, tab.shape[1]), jnp.bfloat16)
    live_count = jnp.sum(
        jnp.where(entries_ref[...] >= 0, 1.0, 0.0), axis=1, keepdims=True
    ).astype(jnp.int32)

    def in_group(rows):
        c = cells_ref[rows, :]
        return c, quot(c[:, 0:1], GROUP)

    def one(g, carry):
        at = pl.multiple_of(g * BATCH, BATCH)
        rows = pl.ds(at, BATCH)
        c, q = in_group(rows)
        x = quot(q, groups)
        key = (q - x * groups) * width + x
        lane = lax.broadcasted_iota(jnp.int32, (BATCH, hot.shape[1]), 1)
        chosen = jnp.where(lane == key, 1.0, 0.0).astype(jnp.bfloat16)
        hot[rows, :] = chosen
        both = jnp.dot(chosen, tab[...], preferred_element_type=jnp.float32)
        offset = c - q * GROUP
        part = offset >> 7
        within = offset & (LANES - 1)

        def look(f):
            high = both[:, 2 * f * GROUP : (2 * f + 1) * GROUP]
            value = high + both[:, (2 * f + 1) * GROUP : (2 * f + 2) * GROUP]
            got = jnp.take_along_axis(value[:, :LANES], within, axis=1)
            for t in range(1, SPAN):
                tile = value[:, t * LANES : (t + 1) * LANES]
                got = jnp.where(part == t, jnp.take_along_axis(tile, within, axis=1), got)
            return got

        theta, vapour = look(0), look(1)
        supersat = vapour - 0.5 * jnp.tanh(theta)
        growth_rate = 1.0 / (1.0 + 0.1 * theta * theta)
        start = drops[0, rows, :]
        solute = drops[1, rows, :]
        weight = drops[2, rows, :]
        square = start * start
        for _ in range(SUBSTEPS):
            radius = jnp.sqrt(square)
            square = jnp.maximum(
                square
                + 0.05
                * growth_rate
                * (supersat - 0.02 / radius + solute / (radius * radius * radius)),
                0.04,
            )
        radius = jnp.sqrt(square)
        radius_out[rows, :] = radius
        grown = weight * (radius * square - start * start * start)
        block = at + lax.broadcasted_iota(jnp.int32, (BATCH, LANES), 0)
        mass[rows, :] = jnp.where(block < live_count, grown, 0.0)
        return carry

    lax.fori_loop(0, plan.home_cap // BATCH, one, 0)


def condense(plan, cells_ref, hot, mass, spread, cond):
    width = plan.width
    groups = plan.merged // GROUP
    row = lax.broadcasted_iota(jnp.int32, (LANES, LANES), 0)
    column = lax.broadcasted_iota(jnp.int32, (LANES, LANES), 1)
    upper = (row <= column).astype(jnp.float32)
    mass[...] = jnp.dot(
        mass[...], upper, precision=lax.Precision.HIGHEST, preferred_element_type=jnp.float32
    )
    lane = lax.broadcasted_iota(jnp.int32, (BATCH, LANES), 1)

    def sums(g, carry):
        rows = pl.ds(pl.multiple_of(g * BATCH, BATCH), BATCH)
        c = cells_ref[rows, :]
        offset = c - quot(c[:, 0:1], GROUP) * GROUP
        column = quot(offset[:, 0:1], NZ)
        level = offset - column * NZ
        count = jnp.zeros((BATCH, LANES), jnp.int32)
        step = LANES
        while step >= 1:
            probe = jnp.minimum(count + (step - 1), LANES - 1)
            below = jnp.take_along_axis(level, probe, axis=1) <= lane
            count = jnp.where(below & (count + step <= LANES), count + step, count)
            step //= 2
        upto = jnp.take_along_axis(mass[rows, :], jnp.maximum(count - 1, 0), axis=1)
        upto = jnp.where(count > 0, upto, 0.0)
        before = jnp.where(lane == 0, 0.0, pltpu.roll(upto, 1, 1))
        picked = upto - before
        for t in range(SPAN):
            place = lane + t * LANES
            which = quot(place, NZ)
            here = jnp.take_along_axis(picked, place - which * NZ, axis=1)
            high, low = split(jnp.where(which == column, here, 0.0))
            spread[rows, t * LANES : (t + 1) * LANES] = high
            spread[rows, GROUP + t * LANES : GROUP + (t + 1) * LANES] = low
        return carry

    lax.fori_loop(0, plan.home_cap // BATCH, sums, 0)
    both = lax.dot_general(
        hot[...], spread[...], (((0,), (0,)), ((), ())), preferred_element_type=jnp.float32
    )
    for g in range(groups):
        rows = slice(g * width, (g + 1) * width)
        cond[:, g * GROUP : (g + 1) * GROUP] = both[rows, :GROUP] + both[rows, GROUP:]


def main_kernel(
    plan,
    entries_ref,
    cells_ref,
    fields_hbm,
    winds_hbm,
    diff_hbm,
    planes_hbm,
    fields_hbm_out,
    drops_hbm_out,
    radius_out,
    lists_hbm_out,
    flag_out,
    fields_out,
    drops_out,
    out_sem,
    ext,
    mid,
    coef,
    cond,
    drops,
    lists,
    pack_hot,
    relay_hot,
    place_hot,
    tab,
    hot,
    mass,
    spread,
    x_send,
    x_recv,
    y_send,
    y_recv,
    load_sem,
    grid_sem,
    list_sem,
    halo_send,
    halo_recv,
    *chunk_refs,
):
    devices, across, along = plan.devices, plan.across, plan.along
    low, levels, places = plan.low, plan.levels, plan.places
    direct, extra, room = plan.direct, plan.extra, plan.room
    width, merged = plan.width, plan.merged
    count = len(CHUNKS)
    per = 6 if extra else 2
    buffers = [chunk_refs[i * per : (i + 1) * per] for i in range(count)]
    sems = chunk_refs[count * per :]
    gx = lax.axis_index("gx")
    gy = lax.axis_index("gy")
    me = gx * along + gy
    my_level = gy // low
    my_place = gx * low + gy % low
    barrier = pltpu.get_barrier_semaphore()

    def device(d):
        return {"gx": d // along, "gy": d % along}

    def greet(s, carry):
        other = (me + s) % devices
        pl.semaphore_signal(barrier, inc=1, device_id=device(other), device_id_type=MESH)
        return carry

    lax.fori_loop(1, devices, greet, 0)

    loads = []
    for i, (at, n) in enumerate(LOADS):
        rows = pl.ds(at, n)
        loads.append(pltpu.make_async_copy(planes_hbm.at[rows], drops.at[rows], load_sem.at[i]))
    own_rows = pl.ds(ROW0, width)
    own_lanes = pl.ds(LANES, merged)
    grids = (
        pltpu.make_async_copy(
            fields_hbm, ext.at[pl.ds(0, 5), own_rows, own_lanes], grid_sem.at[0]
        ),
        pltpu.make_async_copy(winds_hbm, ext.at[pl.ds(5, 3), own_rows, own_lanes], grid_sem.at[1]),
        pltpu.make_async_copy(diff_hbm, ext.at[8, own_rows, own_lanes], grid_sem.at[2]),
    )
    loads[0].start()
    for grid in grids:
        grid.start()
    loads[1].start()
    loads[2].start()

    pack_hot[...] = onehot_rows(send_positions(plan, entries_ref[...]), plan.slots)
    pl.semaphore_wait(barrier, devices - 1)

    def remote(src, dst, send_sem, recv_sem, to):
        return pltpu.make_async_remote_copy(
            src_ref=src,
            dst_ref=dst,
            send_sem=send_sem,
            recv_sem=recv_sem,
            device_id=to,
            device_id_type=MESH,
        )

    halos = []

    def halo(src, dst, dx, dy):
        i = len(halos)
        to = {"gx": (gx + dx + across) % across, "gy": (gy + dy + along) % along}
        copy = remote(src, dst, halo_send.at[i], halo_recv.at[i], to)
        copy.start()
        halos.append(copy)

    left_lanes = pl.ds(0, LANES)
    right_lanes = pl.ds(LANES + merged, LANES)
    begin, end = pl.ds(0, LANES), pl.ds(merged - LANES, LANES)

    def y_halos():
        for grid in grids:
            grid.wait()
        rows = slice(ROW0, ROW0 + width)
        for side, dy in ((0, -1), (1, 1)):
            pieces = []
            for k, n in Y_EDGE:
                at = LANES if side == 0 else LANES + merged - n * NZ
                pieces.append(ext[k, rows, at : at + n * NZ])
            y_send[side] = jnp.concatenate(pieces, axis=1)
            halo(y_send.at[side], y_recv.at[1 - side], 0, dy)

    def y_arrived():
        rows = slice(ROW0, ROW0 + width)
        for side in range(2):
            edge = y_recv[side]
            at = 0
            for k, n in Y_EDGE:
                to = LANES - n * NZ if side == 0 else LANES + merged
                ext[k, rows, to : to + n * NZ] = edge[:, at : at + n * NZ]
                at += n * NZ

    def x_halos():
        for k in range(9):
            x_send[0, k] = ext[k, ROW0 : ROW0 + 2, LANES : LANES + merged]
            x_send[1, k] = ext[k, ROW0 + width - 2 : ROW0 + width, LANES : LANES + merged]
        every, both = pl.ds(0, 9), pl.ds(0, 2)
        for side, dx in ((0, -1), (1, 1)):
            to = x_recv.at[1 - side]
            halo(x_send.at[side], to.at[every, both, own_lanes], dx, 0)
            halo(x_send.at[side, every, both, begin], to.at[every, both, right_lanes], dx, -1)
            halo(x_send.at[side, every, both, end], to.at[every, both, left_lanes], dx, 1)

    my_lists = pl.ds(my_place * levels, levels)

    def tell_levels(s, carry):
        level = (my_level + s) % levels
        to = {"gx": gx, "gy": level * low + gy % low}
        at = lists.at[my_place * levels + my_level]
        remote(entries_ref, at, list_sem.at[0], list_sem.at[1], to).start()
        return carry

    def tell_places(s, carry):
        place = (my_place + s) % places
        to = {"gx": place // low, "gy": my_level * low + place % low}
        mine = lists.at[my_lists]
        remote(mine, mine, list_sem.at[2], list_sem.at[3], to).start()
        return carry

    def pack(c):
        near, far = buffers[c][0], buffers[c][2] if extra else None
        for r, attribute in enumerate(CHUNKS[c]):
            if attribute == 0:
                value = radius_out[...]
            else:
                value = drops[attribute]
                if 3 <= attribute < 6:
                    value = value + 0.1 * drops[attribute + 3]
            packed = pick(pack_hot[...], value)
            cut = devices * direct
            near[:, r * direct : (r + 1) * direct, :] = packed[:cut].reshape(
                devices, direct, LANES
            )
            if extra:
                n = levels * extra
                far[:, r * n : (r + 1) * n, :] = packed[cut:].reshape(places, n, LANES)

    def send(c):
        near, near_in = buffers[c][0:2]
        if extra:
            far, far_in = buffers[c][2:4]

            def give(s, carry):
                place = (my_place + s) % places
                to = {"gx": place // low, "gy": my_level * low + place % low}
                remote(
                    far.at[place], far_in.at[my_place], sems[2].at[c], sems[3].at[c], to
                ).start()
                return carry

            lax.fori_loop(1, places, give, 0)
            far_in[my_place] = far[my_place]

        def out(s, carry):
            other = (me + s) % devices
            remote(
                near.at[other], near_in.at[me], sems[0].at[c], sems[1].at[c], device(other)
            ).start()
            return carry

        lax.fori_loop(1, devices, out, 0)
        near_in[me] = near[me]

    def wait_all(ref, n, sem):
        part = ref.at[pl.ds(0, n)]
        pltpu.make_async_copy(part, part, sem).wait()

    def relay(c):
        far_in, onward, onward_in = buffers[c][3:6]
        wait_all(far_in, places - 1, sems[3].at[c])
        n = levels * extra
        for r in range(len(CHUNKS[c])):
            rows = far_in[:, r * n : (r + 1) * n, :].reshape(places * n, LANES)
            onward[:, r * room : (r + 1) * room, :] = pick(relay_hot[...], rows).reshape(
                levels, room, LANES
            )

        def pass_on(s, carry):
            level = (my_level + s) % levels
            to = {"gx": gx, "gy": level * low + gy % low}
            remote(
                onward.at[level], onward_in.at[my_level], sems[4].at[c], sems[5].at[c], to
            ).start()
            return carry

        lax.fori_loop(1, levels, pass_on, 0)
        onward_in[my_level] = jnp.zeros(onward_in.shape[1:], jnp.float32)

    loads[0].wait()
    lists[my_place * levels + my_level] = entries_ref[...]
    lax.fori_loop(1, levels, tell_levels, 0)
    pack(0)
    send(0)
    y_halos()
    x_halos()
    loads[1].wait()
    loads[2].wait()
    pack(1)
    send(1)
    wait_all(lists, levels - 1, list_sem.at[1])
    lax.fori_loop(1, places, tell_places, 0)
    grow_drops(plan, entries_ref, cells_ref, ext, drops, tab, hot, radius_out, mass)
    pack(2)
    send(2)
    condense(plan, cells_ref, hot, mass, spread, cond)

    for copy in halos:
        copy.wait()
    y_arrived()
    for k in range(9):
        ext[k, ROW0 - 2 : ROW0, :] = x_recv[0, k]
        ext[k, ROW0 + width : ROW0 + width + 2, :] = x_recv[1, k]
    coefficients, advance_once, advance_twice = stencil(plan, ext, mid, coef, cond, fields_out)
    coefficients()

    wait_all(lists, (places - 1) * levels, list_sem.at[3])

    def list_of(d):
        place = (d // along) * low + d % low
        return lists[place * levels + (d % along) // low]

    known = jnp.concatenate([list_of(d) for d in range(devices)], axis=0)
    lists_copy = pltpu.make_async_copy(lists, lists_hbm_out, list_sem.at[4])
    lists_copy.start()
    if extra:
        relay_hot[...] = relay_matrix(plan, known, my_level, my_place)
        relay(0)
        relay(1)
    advance_once()
    if extra:
        relay(2)
    place_hot[...] = arrival_matrix(plan, known, me, my_level)
    advance_twice()
    finished = []

    def finish(which, src, dst, i):
        copy = pltpu.make_async_copy(src.at[i], dst.at[i], out_sem.at[which, i])
        copy.start()
        finished.append(copy)

    for f in range(5):
        finish(0, fields_out, fields_hbm_out, f)

    if extra:
        flag = jnp.zeros((devices, 1), jnp.float32)
        totals = [flag] * levels
        owner = lax.broadcasted_iota(jnp.int32, (devices, plan.home_cap), 0)
        for d in range(devices):
            counts = column_sum(jnp.where((list_of(d) >> OWN_SHIFT) == owner, 1.0, 0.0))
            level = (d % along) // low
            totals[level] = totals[level] + jnp.maximum(counts - direct, 0.0)
        for total in totals:
            flag = jnp.maximum(flag, jnp.where(total > room, 1.0, 0.0))
        flag_out[0] = jnp.max(flag).astype(jnp.int32)
    else:
        flag_out[0] = 0

    for c in range(count):
        near_in = buffers[c][1]
        wait_all(near_in, devices - 1, sems[1].at[c])
        if extra:
            far_in, onward_in = buffers[c][3], buffers[c][5]
            wait_all(onward_in, levels - 1, sems[5].at[c])
        for r, attribute in enumerate(CHUNKS[c]):
            parts = [
                near_in[:, r * direct : (r + 1) * direct, :].reshape(devices * direct, LANES)
            ]
            if extra:
                at = pl.multiple_of((r * levels + my_level) * extra, 8)
                parts.append(far_in[:, pl.ds(at, extra), :].reshape(places * extra, LANES))
                parts.append(
                    onward_in[:, r * room : (r + 1) * room, :].reshape(levels * room, LANES)
                )
            if plan.padded > plan.arrivals:
                parts.append(jnp.zeros((plan.padded - plan.arrivals, LANES), jnp.float32))
            rows = jnp.concatenate(parts, axis=0) if len(parts) > 1 else parts[0]
            drops_out[attribute] = pick(place_hot[...], rows)
            finish(1, drops_out, drops_hbm_out, attribute)

    for copy in finished:
        copy.wait()
    lists_copy.wait()
    wait_all(lists, levels - 1, list_sem.at[0])
    wait_all(lists, (places - 1) * levels, list_sem.at[2])
    for c in range(count):
        wait_all(buffers[c][0], devices - 1, sems[0].at[c])
        if extra:
            wait_all(buffers[c][2], places - 1, sems[2].at[c])
            wait_all(buffers[c][4], levels - 1, sems[4].at[c])


def run_main(plan, entries, cells, fields, winds, diffusion, planes):
    width, merged, home_cap = plan.width, plan.merged, plan.home_cap
    tall = ROW0 + width + 16
    wide = merged + 2 * LANES
    groups = merged // GROUP
    keys = -(-groups * width // LANES) * LANES
    f32, bf16 = jnp.float32, jnp.bfloat16
    buffers = []
    for chunk in CHUNKS:
        n = len(chunk)
        near = pltpu.VMEM((plan.devices, n * plan.direct, LANES), f32)
        buffers += [near, near]
        if plan.extra:
            far = pltpu.VMEM((plan.places, n * plan.levels * plan.extra, LANES), f32)
            onward = pltpu.VMEM((plan.levels, n * plan.room, LANES), f32)
            buffers += [far, far, onward, onward]
    sem = pltpu.SemaphoreType.DMA((len(CHUNKS),))
    relay_shape = (16, LANES)
    if plan.extra:
        relay_shape = (plan.levels * plan.room, plan.places * plan.levels * plan.extra)
    return pl.pallas_call(
        lambda *refs: main_kernel(plan, *refs),
        out_shape=(
            jax.ShapeDtypeStruct(fields.shape, f32),
            jax.ShapeDtypeStruct((planes.shape[0], OWN_BLK, LANES), f32),
            jax.ShapeDtypeStruct((home_cap, LANES), f32),
            jax.ShapeDtypeStruct((plan.devices, 1, home_cap), jnp.int32),
            jax.ShapeDtypeStruct((1,), jnp.int32),
        ),
        in_specs=[VMEM, VMEM, ANY, ANY, ANY, ANY],
        out_specs=(ANY, ANY, VMEM, ANY, SMEM),
        scratch_shapes=[
            pltpu.VMEM(fields.shape, f32),
            pltpu.VMEM((planes.shape[0], OWN_BLK, LANES), f32),
            pltpu.SemaphoreType.DMA((2, max(planes.shape[0], fields.shape[0]))),
            pltpu.VMEM((9, tall, wide), f32),
            pltpu.VMEM((5, tall, wide), f32),
            pltpu.VMEM((7, tall, wide), f32),
            pltpu.VMEM((width, merged), f32),
            pltpu.VMEM(planes.shape, f32),
            pltpu.VMEM((plan.devices, 1, home_cap), jnp.int32),
            pltpu.VMEM((plan.slots, home_cap), bf16),
            pltpu.VMEM(relay_shape, bf16),
            pltpu.VMEM((OWN_BLK, plan.padded), bf16),
            pltpu.VMEM((keys, 4 * GROUP), bf16),
            pltpu.VMEM((home_cap, keys), bf16),
            pltpu.VMEM((home_cap, LANES), f32),
            pltpu.VMEM((home_cap, 2 * GROUP), bf16),
            pltpu.VMEM((2, 9, 2, merged), f32),
            pltpu.VMEM((2, 9, 2, wide), f32),
            pltpu.VMEM((2, width, sum(n for _, n in Y_EDGE) * NZ), f32),
            pltpu.VMEM((2, width, sum(n for _, n in Y_EDGE) * NZ), f32),
            pltpu.SemaphoreType.DMA((len(LOADS),)),
            pltpu.SemaphoreType.DMA((3,)),
            pltpu.SemaphoreType.DMA((5,)),
            pltpu.SemaphoreType.DMA((8,)),
            pltpu.SemaphoreType.DMA((8,)),
            *buffers,
            *([sem] * (6 if plan.extra else 2)),
        ],
        compiler_params=pltpu.CompilerParams(
            vmem_limit_bytes=LIMIT, collective_id=0, has_side_effects=True
        ),
        cost_estimate=cost(16 << 20, 1 << 28),
        name="condense_advance",
    )(entries, cells, fields, winds, diffusion, planes)


def hand_kernel(fields_ref, drops_ref, fields_out, drops_out, fields_held, drops_held, sem):
    arrays = ((fields_ref, fields_held, fields_out), (drops_ref, drops_held, drops_out))
    pieces = [(a, i) for a in arrays for i in range(a[0].shape[0])]

    def move(n, step):
        refs, i = pieces[n]
        return pltpu.make_async_copy(refs[step].at[i], refs[step + 1].at[i], sem.at[step, n])

    for n in range(len(pieces)):
        move(n, 0).start()
    for n in range(len(pieces)):
        move(n, 0).wait()
        move(n, 1).start()
    for n in range(len(pieces)):
        move(n, 1).wait()


def hand_over(fields, drops):
    return pl.pallas_call(
        hand_kernel,
        out_shape=(
            jax.ShapeDtypeStruct(fields.shape, jnp.float32),
            jax.ShapeDtypeStruct(drops.shape, jnp.float32),
        ),
        in_specs=[ANY, ANY],
        out_specs=(ANY, ANY),
        scratch_shapes=[
            pltpu.VMEM(fields.shape, jnp.float32),
            pltpu.VMEM(drops.shape, jnp.float32),
            pltpu.SemaphoreType.DMA((2, fields.shape[0] + drops.shape[0])),
        ],
        compiler_params=pltpu.CompilerParams(vmem_limit_bytes=LIMIT),
        cost_estimate=cost(8 << 20, 1 << 10),
        name="hand_over",
    )(fields, drops)


def resend(plan, balance_list, planes, radius, lists):
    everyone = ("gx", "gy")
    devices, cap = plan.devices, plan.cap
    count = planes.shape[0]

    def exchange(x):
        return lax.all_to_all(x, everyone, split_axis=0, concat_axis=0, tiled=True)

    outgoing = pack_drops(
        balance_list.reshape(1, plan.home_cap),
        jnp.concatenate([planes, radius[None]], axis=0),
        devices,
        cap,
    )
    lists = lists.reshape(plan.across, plan.low, plan.levels, plan.home_cap)
    lists = lists.transpose(0, 2, 1, 3).reshape(devices, plan.home_cap)
    codes = arrival_codes(lax.axis_index(everyone).reshape(1), lists, cap)
    return place_drops(codes, exchange(outgoing), count)


def per_device(fields, winds, diffusion, droplets, cells, balance_list):
    width = fields.shape[1]
    merged = fields.shape[2]
    home_cap = balance_list.shape[0]
    plan = Plan((lax.axis_size("gx"), lax.axis_size("gy")), home_cap, width, merged)
    planes = droplets.transpose(1, 0, 2)
    fields_out, placed, radius, lists, flag = run_main(
        plan, balance_list.reshape(1, home_cap), cells, fields, winds, diffusion, planes
    )
    fields_out, placed = hand_over(fields_out, placed)
    if plan.extra:
        placed = lax.cond(
            flag[0] > 0,
            lambda: resend(plan, balance_list, planes, radius, lists),
            lambda: placed,
        )
    return (fields_out, placed.transpose(1, 0, 2))


def solution(mesh):
    return jax.shard_map(
        per_device,
        mesh=mesh,
        in_specs=(
            P(None, "gx", "gy"),
            P(None, "gx", "gy"),
            P("gx", "gy"),
            P(("gx", "gy"), None, None),
            P(("gx", "gy"), None),
            P(("gx", "gy")),
        ),
        out_specs=(P(None, "gx", "gy"), P(("gx", "gy"), None, None)),
        check_vma=False,
    )
```
